128 devices in a mesh: gx: 8 (over y, core), gy: 16 (over x, z).
Axes of the slice: x: 4, y: 4, z: 4, core: 2. Of those that a mesh axis runs over, the one named last changes fastest.
Arguments:
- hblocks: float32 [8, 16, 9, 128, 128], P('gx', 'gy'), may hold values from -1 to 1, as said below
- onsite: float32 [8, 16, 128], P('gx', 'gy'), may hold values from -1.5 to 1.5
- pattern: int32 [8, 16, 9], P('gx', 'gy'), may hold values 0 or 1
- slot_code: int32 [8, 16, 6], P('gx', 'gy'), may hold values from 0 to 9, as said below
- basis: bfloat16 [8, 16, 9, 1024, 128], P('gx', 'gy'), may hold values from -0.5 to 0.5
Outputs:
- density: bfloat16 [8, 16, 9, 128, 128], P('gx', 'gy')
- grid_density: float32 [8, 16, 1024], P('gx', 'gy')
The draws below stay inside these ranges and needn't reach their ends.
Inputs may be any that keep to these rules, and one draw needn't show every extreme that they name: `hblocks`: standard deviations differ between block columns. `slot_code`: slot 0 of every column holds 4, the block itself; the next slots hold distinct codes other than 4, and the remaining slots hold 9 (unused). Every column uses 2 or more slots, and in every draw some column uses all 6.
All inputs are finite; a program needn't handle non-finite values. No bound on the sum of `pattern` on one device may be relied on, other than what follows from the above.
Results may differ from the reference program's by a relative error of at most 0.001.
Values may be sent and summed in bfloat16 or wider, within the bound.
A program may use at most 128 MiB of HBM per device.

```python
import jax
import jax.numpy as jnp
from jax import lax

B = 128
SLOTS = 6
G = 1024
POWER_STEPS = 6
SIGN_STEPS = 3
N_GX = 8
N_GY = 16


def draw_hblocks(key, part):
    count = N_GX * N_GY
    rank = jnp.arange(count, dtype=jnp.float32).reshape(N_GX, N_GY)
    level = 0.04 * jnp.exp(jnp.log(3.0) * rank / (count - 1))
    key_a = jax.random.fold_in(key, 0)
    shape = (N_GX, N_GY, 9, B, B)
    values = jnp.clip(jax.random.normal(key_a, shape, jnp.float32), -6.0, 6.0)
    return (values * level[:, :, None, None, None]).astype(jnp.float32)


def draw_slot_code(key, part):
    count = N_GX * N_GY
    key_a, key_b, key_c, key_d = jax.random.split(key, 4)
    filled = jax.random.randint(key_a, (count,), 2, 4)
    larger = jax.random.randint(key_b, (count,), 0, 8) == 0
    filled = jnp.where(larger, SLOTS, filled)
    fullest = jax.random.randint(key_c, (), 0, count)
    filled = jnp.where(jnp.arange(count) == fullest, SLOTS, filled)
    scores = jax.random.randint(key_d, (count, 8), 0, 1 << 20) * 8 + jnp.arange(8, dtype=jnp.int32)[None, :]
    order = jnp.argsort(scores, axis=1).astype(jnp.int32)
    others = jnp.where(order >= 4, order + 1, order)
    chosen = jnp.concatenate([jnp.full((count, 1), 4, jnp.int32), others[:, :SLOTS - 1]], axis=1)
    slot_index = jnp.arange(SLOTS, dtype=jnp.int32)
    codes = jnp.where(slot_index[None, :] < filled[:, None], chosen, 9)
    return codes.reshape(N_GX, N_GY, SLOTS).astype(jnp.int32)


def with_ends(values, own_key, least, largest):
    place = [jax.random.randint(jax.random.fold_in(own_key, axis), (), 0, length) for axis, length in enumerate(values.shape)]
    main_axis = values.shape.index(max(values.shape))
    neighbour = place[:main_axis] + [(place[main_axis] + 1) % values.shape[main_axis]] + place[main_axis + 1:]
    return values.at[tuple(place)].set(least).at[tuple(neighbour)].set(largest)


def steps_of(own_key, shape, cuts, low, largest):
    level = 1.0
    for position, shards_of in cuts:
        draws = jax.random.uniform(jax.random.fold_in(jax.random.fold_in(own_key, 6), position), (shards_of,), jnp.float32, low / len(cuts), largest / len(cuts))
        level = level * jnp.repeat(jnp.exp(draws), shape[position] // shards_of).reshape((-1,) + (1,) * (len(shape) - 1 - position))
    return level


def centred(own_key, shape, scale, bound, cuts=(), kind=jnp.bfloat16):
    entries = jax.random.normal(own_key, shape, jnp.float32) * scale
    if len(cuts) > 0:
        entries = steps_of(own_key, shape, cuts, -0.22, 0.18) * entries
    return jnp.clip(entries, min=-bound, max=bound).astype(kind)


def setup_inputs(seed: int = 0) -> dict:
    splits = jax.random.split(jax.random.key(seed), 6)
    hblocks = draw_hblocks(jax.random.fold_in(splits[5], 71), 0)
    onsite = jnp.clip(jax.random.uniform(splits[1], (N_GX, N_GY, B), jnp.float32, -1.5, 1.5) * steps_of(splits[1], (N_GX, N_GY, B), ((0, 8), (1, 16)), -0.4, 0.0), -1.5, 1.5)
    pattern = with_ends((jax.random.randint(splits[2], (N_GX, N_GY, 9), 0, 4) < 3).astype(jnp.int32), jax.random.fold_in(splits[2], 1), 0, 1)
    slot_code = draw_slot_code(jax.random.fold_in(splits[5], 71), 0)
    basis = centred(splits[4], (N_GX, N_GY, 9, G, B), B ** -0.5, 0.5, ((0, 8), (1, 16)))
    return dict(hblocks=hblocks, onsite=onsite, pattern=pattern, slot_code=slot_code, basis=basis)


HIGH = lax.Precision.HIGHEST

def columns_of(hblocks, onsite, pattern):
    codes = jnp.arange(9, dtype=jnp.int32)
    kept = jnp.where(codes == 4, 1, pattern).astype(jnp.float32)
    masked = hblocks * kept[:, :, :, None, None]
    identity = jnp.eye(hblocks.shape[-1], dtype=jnp.float32)
    diagonal = onsite[:, :, :, None] * identity
    return masked.at[:, :, 4].add(diagonal)

def slot_geometry(codes):
    used = codes < 9
    safe = jnp.where(used, codes, 4)
    offset_x = safe // 3 - 1
    offset_y = safe % 3 - 1
    diff_x = offset_x[:, None] - offset_x[None, :]
    diff_y = offset_y[:, None] - offset_y[None, :]
    valid = (jnp.abs(diff_x) <= 1) & (jnp.abs(diff_y) <= 1) & used[:, None] & used[None, :]
    inner = jnp.clip((diff_x + 1) * 3 + diff_y + 1, 0, 8).astype(jnp.int32)
    return (used, safe, offset_x, offset_y, valid, inner)

def submatrix(columns, codes, xpos, ypos):
    slots = codes.shape[0]
    width = columns.shape[-1]
    used, safe, offset_x, offset_y, valid, inner = slot_geometry(codes)
    source_x = ((xpos + offset_x) % N_GX).astype(jnp.int32)
    source_y = ((ypos + offset_y) % N_GY).astype(jnp.int32)
    grid_x = jnp.broadcast_to(source_x[None, :], (slots, slots))
    grid_y = jnp.broadcast_to(source_y[None, :], (slots, slots))
    blocks = columns[grid_x, grid_y, inner]
    blocks = jnp.where(valid[:, :, None, None], blocks, jnp.float32(0.0))
    matrix = blocks.transpose(0, 2, 1, 3).reshape(slots * width, slots * width)
    return (0.5 * (matrix + matrix.T), used)

def power_bound(matrix, used, width):
    vector = jnp.repeat(used.astype(jnp.float32), width)
    for step in range(POWER_STEPS):
        image = jnp.dot(matrix, vector, precision=HIGH)
        vector = image / jnp.sqrt(jnp.sum(image * image) + 1e-06)
    image = jnp.dot(matrix, vector, precision=HIGH)
    return jnp.sqrt(jnp.sum(image * image) + 1e-06)

def sign_poly(matrix, scale):
    current = matrix / scale
    for step in range(SIGN_STEPS):
        square = jnp.dot(current, current, precision=HIGH)
        current = 1.5 * current - 0.5 * jnp.dot(current, square, precision=HIGH)
    return current

def expand(column, codes, width):
    slots = codes.shape[0]
    first = jnp.eye(slots * width, width, dtype=jnp.float32)
    halves = 0.5 * (first - column)
    onehot = (codes[None, :] == jnp.arange(9, dtype=jnp.int32)[:, None]).astype(jnp.float32)
    spread = jnp.dot(onehot, halves.reshape(slots, width * width), precision=HIGH)
    return spread.reshape(9, width, width).astype(jnp.bfloat16)

def reference(hblocks, onsite, pattern, slot_code, basis):
    width = hblocks.shape[-1]
    points = basis.shape[3]
    columns = columns_of(hblocks, onsite, pattern)
    indices = jnp.arange(N_GX * N_GY, dtype=jnp.int32)

    def estimate_one(index):
        xpos = index // N_GY
        ypos = index % N_GY
        matrix, used = submatrix(columns, slot_code[xpos, ypos], xpos, ypos)
        return power_bound(matrix, used, width)
    estimates = lax.map(estimate_one, indices)
    scale = 1.25 * jnp.max(estimates)

    def density_one(index):
        xpos = index // N_GY
        ypos = index % N_GY
        matrix, used = submatrix(columns, slot_code[xpos, ypos], xpos, ypos)
        column = sign_poly(matrix, scale)[:, :width]
        return expand(column, slot_code[xpos, ypos], width)
    density = lax.map(density_one, indices).reshape(N_GX, N_GY, 9, width, width)

    def tile_one(index):
        xpos = index // N_GY
        ypos = index % N_GY
        total = jnp.zeros((points,), jnp.float32)
        for near in range(9):
            near_x = near // 3 - 1
            near_y = near % 3 - 1
            blocks = density[(xpos + near_x) % N_GX, (ypos + near_y) % N_GY]
            accum = jnp.zeros((points, width), jnp.float32)
            for code in range(9):
                far_x = near_x + code // 3 - 1
                far_y = near_y + code % 3 - 1
                if abs(far_x) <= 1 and abs(far_y) <= 1:
                    accum = accum + jnp.dot(basis[xpos, ypos, (far_x + 1) * 3 + far_y + 1], blocks[code], preferred_element_type=jnp.float32)
            total = total + lax.optimization_barrier(jnp.sum(accum * basis[xpos, ypos, near].astype(jnp.float32), axis=1))
        return total
    grid_density = lax.map(tile_one, indices).reshape(N_GX, N_GY, points)
    return (density, grid_density)
```

```python
import functools

import jax
import jax.numpy as jnp
from jax import lax
from jax.experimental import pallas as pl
from jax.experimental.pallas import tpu as pltpu
from jax.sharding import PartitionSpec as P

POWER_STEPS = 6
B = 128
SLOTS = 6
ORDER = SLOTS * B
MESH = pl.DeviceIdType.MESH
F32 = jnp.float32
BF16 = jnp.bfloat16

BELOW_X, ABOVE_X, BELOW_Y, ABOVE_Y = 1, 7, 3, 5


def needed(place):
    spans = (slice(1, 3), slice(0, 3), slice(0, 2))
    return spans[place // 3], spans[place % 3]


def split(value):
    high = value.astype(BF16)
    return high, (value - high.astype(F32)).astype(BF16)


def exchange(hood, sends, recvs, base, gx, gy, n_gx, n_gy):
    up_x = (lax.rem(gx + 1, n_gx), gy)
    down_x = (lax.rem(gx + n_gx - 1, n_gx), gy)
    up_y = (gx, lax.rem(gy + 1, n_gy))
    down_y = (gx, lax.rem(gy + n_gy - 1, n_gy))

    def copy(index, source, target, rows, columns, device):
        return pltpu.make_async_remote_copy(
            src_ref=hood.at[source, rows, columns],
            dst_ref=hood.at[target, rows, columns],
            send_sem=sends.at[index],
            recv_sem=recvs.at[index],
            device_id=device,
            device_id_type=MESH,
        )

    copies = {}
    index = base
    for row in (1, 0, 2):
        for place, device in ((BELOW_Y, up_y), (ABOVE_Y, down_y)):
            columns = needed(place)[1]
            copies[place, row] = copy(index, 4, place, slice(row, row + 1), columns, device)
            index += 1
    for place, device in ((BELOW_X, up_x), (ABOVE_X, down_x)):
        rows, columns = needed(place)
        copies[place] = copy(index, 4, place, rows, columns, device)
        index += 1
    for row in (1, 0, 2):
        for source in (BELOW_Y, ABOVE_Y):
            for shift, device in ((-1, up_x), (1, down_x)):
                place = source + 3 * shift
                rows, columns = needed(place)
                if rows.start <= row < rows.stop:
                    copies[place, row] = copy(
                        index, source, place, slice(row, row + 1), columns, device
                    )
                    index += 1
    return copies


COPIES = 16


def begin(copies):
    for row in (1, 0, 2):
        for place in (BELOW_Y, ABOVE_Y):
            copies[place, row].start()
    for place in (BELOW_X, ABOVE_X):
        copies[place].start()


def forward(copies, row):
    for source in (BELOW_Y, ABOVE_Y):
        copies[source, row].wait_recv()
        for place in (source - 3, source + 3):
            if (place, row) in copies:
                copies[place, row].start()


def three(left, right):
    lhs = jnp.concatenate([left[0], left[0], left[1]], axis=1)
    rhs = jnp.concatenate([right[0], right[1], right[0]], axis=0)
    return jnp.dot(lhs, rhs, preferred_element_type=F32)


def thin(matrix, high, low):
    rhs = jnp.concatenate([high, low], axis=1)
    out = []
    for start in range(0, ORDER, 256):
        rows = slice(start, start + 256)
        both = jnp.dot(matrix[0][rows, :], rhs, preferred_element_type=F32)
        rest = jnp.dot(matrix[1][rows, :], high, preferred_element_type=F32)
        out.append(both[:, :B] + (both[:, B:] + rest))
    return jnp.concatenate(out, axis=0)


def kernel(
    n_gx, n_gy,
    h_any, onsite_ref, pattern_ref, code_ref, basis_any,
    density_ref, grid_ref,
    h_buf, basis, hood, m_f, m_hi, m_lo, q_hi, q_lo, n_f, x_hi, x_lo,
    column, halves, dhood, grid_acc, best, best_x, best_y,
    in_sem, sends, recvs, sends_x, recvs_x, sends_y, recvs_y,
):
    gx, gy = lax.axis_index("gx"), lax.axis_index("gy")

    load_h = pltpu.make_async_copy(h_any.at[0, 0], h_buf, in_sem.at[0])
    load_h.start()
    barrier = pltpu.get_barrier_semaphore()
    for step in range(1, n_gx):
        pl.semaphore_signal(barrier, inc=1, device_id=(lax.rem(gx + step, n_gx), gy), device_id_type=MESH)
    for step in range(1, n_gy):
        pl.semaphore_signal(barrier, inc=1, device_id=(gx, lax.rem(gy + step, n_gy)), device_id_type=MESH)
    load_h.wait()
    load_basis = pltpu.make_async_copy(basis_any.at[0, 0], basis, in_sem.at[1])
    load_basis.start()

    rows_of = lax.broadcasted_iota(jnp.int32, (B, B), 0)
    columns_of = lax.broadcasted_iota(jnp.int32, (B, B), 1)
    eye = rows_of == columns_of
    for code in range(9):
        block = h_buf[code]
        if code == 4:
            block = block + jnp.where(eye, onsite_ref[0], 0.0)
        else:
            block = block * pattern_ref[0, 0, code].astype(F32)
        high, low = split(block)
        hood[4, code // 3, code % 3, 0] = high
        hood[4, code // 3, code % 3, 1] = low
    pl.semaphore_wait(barrier, n_gx + n_gy - 2)

    copies = exchange(hood, sends, recvs, 0, gx, gy, n_gx, n_gy)
    begin(copies)
    for row in (1, 0, 2):
        forward(copies, row)
    for key in copies:
        if key in (BELOW_X, ABOVE_X) or key[0] not in (BELOW_Y, ABOVE_Y):
            copies[key].wait_recv()

    codes = [code_ref[0, 0, a] for a in range(SLOTS)]
    used = [code < 9 for code in codes]
    safe = [jnp.where(u, code, 4) for u, code in zip(used, codes)]
    off_x = [lax.div(s, 3) - 1 for s in safe]
    off_y = [lax.rem(s, 3) - 1 for s in safe]

    def stored(a, b):
        dx, dy = off_x[a] - off_x[b], off_y[a] - off_y[b]
        valid = (jnp.abs(dx) <= 1) & (jnp.abs(dy) <= 1) & used[a] & used[b]
        source = jnp.where(valid, safe[b], 4)
        row = jnp.where(valid, dx + 1, 1)
        col = jnp.where(valid, dy + 1, 1)
        block = hood[source, row, col, 0].astype(F32) + hood[source, row, col, 1].astype(F32)
        return jnp.where(valid, block, 0.0)

    def put(a, b, block):
        place = (slice(a * B, a * B + B), slice(b * B, b * B + B))
        m_f[place] = block
        high, low = split(block)
        m_hi[place] = high
        m_lo[place] = low

    for a in range(SLOTS):
        block = stored(a, a)
        put(a, a, 0.5 * (block + block.T))
        for b in range(a + 1, SLOTS):
            upper = 0.5 * (stored(a, b) + stored(b, a).T)
            put(a, b, upper)
            put(b, a, upper.T)

    def from_rows(vector):
        out = []
        for b in range(SLOTS):
            total = jnp.zeros((8, B), F32)
            for a in range(SLOTS):
                part = m_f[a * B:a * B + B, b * B:b * B + B] * vector[a]
                total = total + jnp.sum(part.reshape(B // 8, 8, B), axis=0)
            out.append(jnp.sum(total, axis=0, keepdims=True))
        return out

    def from_lanes(vector):
        out = []
        for a in range(SLOTS):
            total = jnp.zeros((B, B), F32)
            for b in range(SLOTS):
                total = total + m_f[a * B:a * B + B, b * B:b * B + B] * vector[b]
            out.append(jnp.sum(total, axis=1, keepdims=True))
        return out

    def norm2(vector):
        total = sum(part * part for part in vector)
        return jnp.sum(total, keepdims=True) + 1e-6

    vector = [jnp.full((B, 1), 1.0, F32) * u.astype(F32) for u in used]
    for step in range(POWER_STEPS + 1):
        image = from_rows(vector) if step % 2 == 0 else from_lanes(vector)
        squares = norm2(image)
        if step < POWER_STEPS:
            factor = lax.rsqrt(squares)
            vector = [part * factor for part in image]
    estimate = jnp.sqrt(squares)
    best[0] = jnp.broadcast_to(estimate, (8, B))

    def share(source, target, sends_to, recvs_to, count, axis):
        out = []
        for step in range(1, count):
            peer = (lax.rem(gx + step, n_gx), gy) if axis == 0 else (gx, lax.rem(gy + step, n_gy))
            out.append(pltpu.make_async_remote_copy(
                src_ref=best.at[source],
                dst_ref=target.at[step - 1],
                send_sem=sends_to.at[step - 1],
                recv_sem=recvs_to.at[step - 1],
                device_id=peer,
                device_id_type=MESH,
            ))
        return out

    along_x = share(0, best_x, sends_x, recvs_x, n_gx, 0)
    along_y = share(1, best_y, sends_y, recvs_y, n_gy, 1)
    for copy in along_x:
        copy.start()

    for r in range(0, ORDER, 256):
        for c in range(0, ORDER, 256):
            rows, cols = slice(r, r + 256), slice(c, c + 256)
            block = three((m_hi[rows, :], m_lo[rows, :]), (m_hi[:, cols], m_lo[:, cols]))
            high, low = split(block)
            q_hi[rows, cols] = high
            q_lo[rows, cols] = low

    top = best[0]
    for step, copy in enumerate(along_x):
        copy.wait_recv()
        top = jnp.maximum(top, best_x[step])
    best[1] = top
    for copy in along_y:
        copy.start()

    for r in range(0, ORDER, 256):
        for c in range(0, ORDER, 256):
            rows, cols = slice(r, r + 256), slice(c, c + 256)
            n_f[rows, cols] = three((m_hi[rows, :], m_lo[rows, :]), (q_hi[:, cols], q_lo[:, cols]))

    powers = [m_f[:, :B], n_f[:, :B]]
    for _ in range(3):
        powers.append(thin((q_hi, q_lo), *split(powers[-1])))

    top = best[1]
    for step, copy in enumerate(along_y):
        copy.wait_recv()
        top = jnp.maximum(top, best_y[step])
    inverse = 1.0 / (1.25 * top[:1, :1])
    square = inverse * inverse

    alpha, beta = 1.5 * inverse, -0.5 * inverse * square
    for r in range(0, ORDER, B):
        rows = slice(r, r + B)
        high, low = split(alpha * m_f[rows, :] + beta * n_f[rows, :])
        x_hi[rows, :] = high
        x_lo[rows, :] = low
    weights = (
        2.25 * inverse,
        inverse * square * (-0.75 - 0.5 * 3.375),
        inverse * square * square * (0.5 * 3.375),
        inverse * square * square * square * (-0.5 * 1.125),
        inverse * square * square * square * square * (0.5 * 0.125),
    )
    second = sum(w * p for w, p in zip(weights, powers))

    def applied(value):
        once = thin((x_hi, x_lo), *split(value))
        twice = thin((x_hi, x_lo), *split(once))
        return 1.5 * once - 0.5 * thin((x_hi, x_lo), *split(twice))

    third = 1.5 * second - 0.5 * applied(applied(second))
    for a in range(SLOTS):
        block = -third[a * B:a * B + B]
        if a == 0:
            block = jnp.where(eye, 1.0, 0.0) + block
        halves[a] = (0.5 * block).astype(BF16)
    for code in range(9):
        slot = jnp.int32(0)
        held = codes[0] == code
        for a in range(1, SLOTS):
            slot = jnp.where(codes[a] == code, a, slot)
            held = held | (codes[a] == code)
        block = jnp.where(held, halves[slot], jnp.zeros((B, B), BF16))
        dhood[4, code // 3, code % 3] = block
        density_ref[0, 0, code] = block

    dcopies = exchange(dhood, sends, recvs, COPIES + 2, gx, gy, n_gx, n_gy)
    begin(dcopies)
    load_basis.wait()

    def tile(place, first):
        near_x, near_y = place // 3 - 1, place % 3 - 1
        lefts, rights = [], []
        for code in range(9):
            far_x, far_y = near_x + code // 3 - 1, near_y + code % 3 - 1
            if abs(far_x) <= 1 and abs(far_y) <= 1:
                lefts.append((far_x + 1) * 3 + far_y + 1)
                rights.append(dhood[place, code // 3, code % 3])
        right = jnp.concatenate(rights, axis=0)
        for start in range(0, grid_acc.shape[0], 256):
            rows = slice(start, start + 256)
            left = jnp.concatenate([basis[e, rows, :] for e in lefts], axis=1)
            product = jnp.dot(left, right, preferred_element_type=F32)
            product = product * basis[place, rows, :].astype(F32)
            if first:
                grid_acc[rows, :] = product
            else:
                grid_acc[rows, :] = grid_acc[rows, :] + product

    tile(4, True)
    for row in (1, 0, 2):
        forward(dcopies, row)
    for place in (BELOW_Y, ABOVE_Y):
        tile(place, False)
    for place in (BELOW_X, ABOVE_X):
        dcopies[place].wait_recv()
        tile(place, False)
    for place in (0, 2, 6, 8):
        for row in range(3):
            if (place, row) in dcopies:
                dcopies[place, row].wait_recv()
        tile(place, False)
    for part in range(grid_acc.shape[0] // B):
        block = grid_acc[part * B:part * B + B, :]
        grid_ref[0, 0, pl.ds(part * B, B)] = jnp.sum(block.T, axis=0)

    for group in (copies, dcopies):
        for key in group:
            group[key].wait_send()
    for copy in along_x + along_y:
        copy.wait_send()


def local(n_gx, n_gy, hblocks, onsite, pattern, slot_code, basis):
    points = basis.shape[3]
    total = COPIES + 2
    any_space = pl.BlockSpec(memory_space=pl.ANY)
    vmem = pl.BlockSpec(memory_space=pltpu.VMEM)
    smem = pl.BlockSpec(memory_space=pltpu.SMEM)
    square = (ORDER, ORDER)
    return pl.pallas_call(
        functools.partial(kernel, n_gx, n_gy),
        out_shape=(
            jax.ShapeDtypeStruct((1, 1, 9, B, B), BF16),
            jax.ShapeDtypeStruct((1, 1, points), F32),
        ),
        in_specs=[any_space, vmem, smem, smem, any_space],
        out_specs=(vmem, vmem),
        scratch_shapes=[
            pltpu.VMEM((9, B, B), F32),
            pltpu.VMEM((9, points, B), BF16),
            pltpu.VMEM((9, 3, 3, 2, B, B), BF16),
            pltpu.VMEM(square, F32),
            pltpu.VMEM(square, BF16),
            pltpu.VMEM(square, BF16),
            pltpu.VMEM(square, BF16),
            pltpu.VMEM(square, BF16),
            pltpu.VMEM(square, F32),
            pltpu.VMEM(square, BF16),
            pltpu.VMEM(square, BF16),
            pltpu.VMEM((SLOTS, B, B), F32),
            pltpu.VMEM((SLOTS, B, B), BF16),
            pltpu.VMEM((9, 3, 3, B, B), BF16),
            pltpu.VMEM((points, B), F32),
            pltpu.VMEM((2, 8, B), F32),
            pltpu.VMEM((n_gx - 1, 8, B), F32),
            pltpu.VMEM((n_gy - 1, 8, B), F32),
            pltpu.SemaphoreType.DMA((2,)),
            pltpu.SemaphoreType.DMA((2 * total,)),
            pltpu.SemaphoreType.DMA((2 * total,)),
            pltpu.SemaphoreType.DMA((n_gx - 1,)),
            pltpu.SemaphoreType.DMA((n_gx - 1,)),
            pltpu.SemaphoreType.DMA((n_gy - 1,)),
            pltpu.SemaphoreType.DMA((n_gy - 1,)),
        ],
        compiler_params=pltpu.CompilerParams(
            collective_id=0, has_side_effects=True, vmem_limit_bytes=60 << 20
        ),
    )(hblocks, onsite, pattern, slot_code, basis)


def solution(mesh):
    placed = (
        P("gx", "gy", None, None, None),
        P("gx", "gy", None),
        P("gx", "gy", None),
        P("gx", "gy", None),
        P("gx", "gy", None, None, None),
    )
    return jax.shard_map(
        functools.partial(local, mesh.shape["gx"], mesh.shape["gy"]),
        mesh=mesh,
        in_specs=placed,
        out_specs=(P("gx", "gy", None, None, None), P("gx", "gy", None)),
        check_vma=False,
    )
```

```python
import functools

import jax
import jax.numpy as jnp
from jax import lax
from jax.experimental import pallas as pl
from jax.experimental.pallas import tpu as pltpu
from jax.sharding import PartitionSpec as P

POWER_STEPS = 6
B = 128
SLOTS = 6
ORDER = SLOTS * B
MESH = pl.DeviceIdType.MESH
F32 = jnp.float32
BF16 = jnp.bfloat16

BELOW_X, ABOVE_X, BELOW_Y, ABOVE_Y = 1, 7, 3, 5
COPIES = 18

HIGH = 1
LOW = (0, 5, 4)


def split(value):
    high = value.astype(BF16)
    return high, (value - high.astype(F32)).astype(BF16)


class Exchange:
    def __init__(self, hood, sends, recvs, base, gx, gy, n_gx, n_gy, lows):
        odd = lax.rem(gx, 2)
        up_y = (gx, lax.rem(gy + 1, n_gy))
        down_y = (gx, lax.rem(gy + n_gy - 1, n_gy))
        step = 2 * odd - 1
        far = (lax.rem(gx + step + n_gx, n_gx), gy)
        near = (gx - step, gy)
        self.index = base

        def copy(source, target, rows, columns, device):
            index = self.index
            self.index += 1
            return pltpu.make_async_remote_copy(
                src_ref=hood.at[source, rows, columns],
                dst_ref=hood.at[target, rows, columns],
                send_sem=sends.at[index],
                recv_sem=recvs.at[index],
                device_id=device,
                device_id_type=MESH,
            )

        if lows:
            wide = {BELOW_Y: slice(2, 5), ABOVE_Y: slice(0, 3)}
            slim = {BELOW_Y: slice(2, 4), ABOVE_Y: slice(1, 3)}
            across = slice(1, 4)
        else:
            wide = slim = {BELOW_Y: slice(1, 3), ABOVE_Y: slice(0, 2)}
            across = slice(0, 3)
        towards_far = pl.ds(2 * odd, 1)
        towards_near = pl.ds(2 - 2 * odd, 1)
        middle = pl.ds(1, 1)
        self.along_y = []
        self.onward = []
        sides = ((BELOW_Y, up_y), (ABOVE_Y, down_y))
        for rows in (middle, towards_far, towards_near):
            self.along_y.append([copy(4, place, rows, wide[place], device) for place, device in sides])
        self.along_x = [
            copy(4, 4 - 3 * step, pl.ds(odd, 2), across, far),
            copy(4, 4 + 3 * step, pl.ds(1 - odd, 2), across, near),
        ]
        if lows:
            single = slice(LOW[1], LOW[1] + 1)
            self.along_x += [
                copy(4, 4 - 3 * step, towards_far, single, far),
                copy(4, 4 + 3 * step, towards_near, single, near),
            ]
        for rows, columns, targets in (
            (middle, slim, ((far, -3 * step), (near, 3 * step))),
            (towards_far, wide, ((far, -3 * step),)),
            (towards_near, wide, ((near, 3 * step),)),
        ):
            self.onward.append([
                [copy(source, source + shift, rows, columns[source], device) for device, shift in targets]
                for source in (BELOW_Y, ABOVE_Y)
            ])

    def begin_row(self, order):
        for copy in self.along_y[order]:
            copy.start()

    def begin_x(self):
        for copy in self.along_x:
            copy.start()

    def forward(self, order):
        for arriving, going in zip(self.along_y[order], self.onward[order]):
            arriving.wait_recv()
            for copy in going:
                copy.start()

    def wait_x(self):
        for copy in self.along_x:
            copy.wait_recv()

    def wait_onward(self):
        for order in self.onward:
            for going in order:
                for copy in going:
                    copy.wait_recv()

    def wait_sent(self):
        for group in self.along_y:
            for copy in group:
                copy.wait_send()
        for copy in self.along_x:
            copy.wait_send()
        for order in self.onward:
            for going in order:
                for copy in going:
                    copy.wait_send()


def three(left, right):
    lhs = jnp.concatenate([left[0], left[0], left[1]], axis=1)
    rhs = jnp.concatenate([right[0], right[1], right[0]], axis=0)
    return jnp.dot(lhs, rhs, preferred_element_type=F32)


def thin(matrix, high, low):
    rhs = jnp.concatenate([high, low], axis=1)
    out = []
    for start in range(0, ORDER, 256):
        rows = slice(start, start + 256)
        both = jnp.dot(matrix[0][rows, :], rhs, preferred_element_type=F32)
        rest = jnp.dot(matrix[1][rows, :], high, preferred_element_type=F32)
        out.append(both[:, :B] + (both[:, B:] + rest))
    return jnp.concatenate(out, axis=0)


def kernel(
    n_gx, n_gy,
    h_any, onsite_any, pattern_any, code_any, basis_any,
    density_ref, grid_ref,
    h_buf, onsite_ref, pattern_ref, code_ref, basis, hood, m_f, m_hi, m_lo, q_hi, q_lo, n_f, x_hi, x_lo,
    halves, dhood, grid_acc, best, best_x, best_y,
    in_sem, sends, recvs, sends_x, recvs_x, sends_y, recvs_y,
):
    gx, gy = lax.axis_index("gx"), lax.axis_index("gy")

    barrier = pltpu.get_barrier_semaphore()
    for step in range(1, n_gx):
        pl.semaphore_signal(barrier, inc=1, device_id=(lax.rem(gx + step, n_gx), gy), device_id_type=MESH)
    for step in range(1, n_gy):
        pl.semaphore_signal(barrier, inc=1, device_id=(gx, lax.rem(gy + step, n_gy)), device_id_type=MESH)
    loads = []
    for order, row in enumerate((1, 0, 2)):
        rows = pl.ds(3 * row, 3)
        loads.append(pltpu.make_async_copy(h_any.at[0, 0, rows], h_buf.at[rows], in_sem.at[order]))
        loads[-1].start()
        if order == 0:
            load_pattern = pltpu.make_async_copy(pattern_any, pattern_ref, in_sem.at[4])
            load_onsite = pltpu.make_async_copy(onsite_any, onsite_ref, in_sem.at[5])
            load_codes = pltpu.make_async_copy(code_any, code_ref, in_sem.at[6])
            load_pattern.start()
            load_onsite.start()
            load_codes.start()
    load_basis = pltpu.make_async_copy(basis_any.at[0, 0], basis, in_sem.at[3])
    load_basis.start()

    rows_of = lax.broadcasted_iota(jnp.int32, (B, B), 0)
    columns_of = lax.broadcasted_iota(jnp.int32, (B, B), 1)
    eye = rows_of == columns_of

    def prepare(row):
        for col in range(3):
            code = 3 * row + col
            block = h_buf[code]
            if code == 4:
                block = block + jnp.where(eye, onsite_ref[0], 0.0)
            else:
                block = block * pattern_ref[0, 0, code].astype(F32)
            high, low = split(block)
            hood[4, row, HIGH + col] = high
            hood[4, row, LOW[col]] = low

    swap = Exchange(hood, sends, recvs, 0, gx, gy, n_gx, n_gy, True)
    load_pattern.wait()
    load_onsite.wait()
    load_codes.wait()
    loads[0].wait()
    prepare(1)
    pl.semaphore_wait(barrier, n_gx + n_gy - 2)
    swap.begin_row(0)
    loads[1].wait()
    prepare(0)
    loads[2].wait()
    prepare(2)
    swap.begin_row(1)
    swap.begin_row(2)
    swap.begin_x()
    for order in range(3):
        swap.forward(order)
    swap.wait_x()
    swap.wait_onward()

    codes = [code_ref[0, 0, a] for a in range(SLOTS)]
    used = [code < 9 for code in codes]
    safe = [jnp.where(u, code, 4) for u, code in zip(used, codes)]
    off_x = [lax.div(s, 3) - 1 for s in safe]
    off_y = [lax.rem(s, 3) - 1 for s in safe]

    def stored(a, b):
        dx, dy = off_x[a] - off_x[b], off_y[a] - off_y[b]
        valid = (jnp.abs(dx) <= 1) & (jnp.abs(dy) <= 1) & used[a] & used[b]
        source = jnp.where(valid, safe[b], 4)
        row = jnp.where(valid, dx + 1, 1)
        col = jnp.where(valid, dy + 1, 1)
        block = hood[source, row, col + HIGH].astype(F32)
        if a == 0 or b == 0:
            plane = jnp.where(col == 1, LOW[1], jnp.where(col == 0, LOW[0], LOW[2]))
            block = block + hood[source, row, plane].astype(F32)
        return jnp.where(valid, block, 0.0)

    def put(a, b, block):
        place = (slice(a * B, a * B + B), slice(b * B, b * B + B))
        m_f[place] = block
        high, low = split(block)
        m_hi[place] = high
        m_lo[place] = low

    for a in range(SLOTS):
        block = stored(a, a)
        put(a, a, 0.5 * (block + block.T))
        for b in range(a + 1, SLOTS):
            upper = 0.5 * (stored(a, b) + stored(b, a).T)
            put(a, b, upper)
            put(b, a, upper.T)

    def from_rows(vector):
        out = []
        for b in range(SLOTS):
            total = jnp.zeros((8, B), F32)
            for a in range(SLOTS):
                part = m_f[a * B:a * B + B, b * B:b * B + B] * vector[a]
                total = total + jnp.sum(part.reshape(B // 8, 8, B), axis=0)
            out.append(jnp.sum(total, axis=0, keepdims=True))
        return out

    def from_lanes(vector):
        out = []
        for a in range(SLOTS):
            total = jnp.zeros((B, B), F32)
            for b in range(SLOTS):
                total = total + m_f[a * B:a * B + B, b * B:b * B + B] * vector[b]
            out.append(jnp.sum(total, axis=1, keepdims=True))
        return out

    def norm2(vector):
        total = sum(part * part for part in vector)
        return jnp.sum(total, keepdims=True) + 1e-6

    vector = [jnp.full((B, 1), 1.0, F32) * u.astype(F32) for u in used]
    for step in range(POWER_STEPS + 1):
        image = from_rows(vector) if step % 2 == 0 else from_lanes(vector)
        squares = norm2(image)
        if step < POWER_STEPS:
            factor = lax.rsqrt(squares)
            vector = [part * factor for part in image]
    estimate = jnp.sqrt(squares)
    best[0] = jnp.broadcast_to(estimate, (8, B))

    def share(source, target, sends_to, recvs_to, count, axis):
        out = []
        for step in range(1, count):
            peer = (lax.rem(gx + step, n_gx), gy) if axis == 0 else (gx, lax.rem(gy + step, n_gy))
            out.append(pltpu.make_async_remote_copy(
                src_ref=best.at[source],
                dst_ref=target.at[step - 1],
                send_sem=sends_to.at[step - 1],
                recv_sem=recvs_to.at[step - 1],
                device_id=peer,
                device_id_type=MESH,
            ))
        return out

    along_x = share(0, best_x, sends_x, recvs_x, n_gx, 0)
    along_y = share(1, best_y, sends_y, recvs_y, n_gy, 1)
    for copy in along_x:
        copy.start()

    for r in range(0, ORDER, 256):
        for c in range(r, ORDER, 256):
            rows, cols = slice(r, r + 256), slice(c, c + 256)
            block = three((m_hi[rows, :], m_lo[rows, :]), (m_hi[:, cols], m_lo[:, cols]))
            high, low = split(block)
            q_hi[rows, cols] = high
            q_lo[rows, cols] = low
            if r != c:
                high, low = split(block.T)
                q_hi[cols, rows] = high
                q_lo[cols, rows] = low

    top = best[0]
    for step, copy in enumerate(along_x):
        copy.wait_recv()
        top = jnp.maximum(top, best_x[step])
    best[1] = top
    for copy in along_y:
        copy.start()

    for r in range(0, ORDER, 256):
        for c in range(r, ORDER, 256):
            rows, cols = slice(r, r + 256), slice(c, c + 256)
            block = three((m_hi[rows, :], m_lo[rows, :]), (q_hi[:, cols], q_lo[:, cols]))
            n_f[rows, cols] = block
            if r != c:
                n_f[cols, rows] = block.T

    powers = [m_f[:, :B], n_f[:, :B]]
    for _ in range(3):
        powers.append(thin((q_hi, q_lo), *split(powers[-1])))

    top = best[1]
    for step, copy in enumerate(along_y):
        copy.wait_recv()
        top = jnp.maximum(top, best_y[step])
    inverse = 1.0 / (1.25 * top[:1, :1])
    square = inverse * inverse

    alpha, beta = 1.5 * inverse, -0.5 * inverse * square
    for r in range(0, ORDER, B):
        rows = slice(r, r + B)
        high, low = split(alpha * m_f[rows, :] + beta * n_f[rows, :])
        x_hi[rows, :] = high
        x_lo[rows, :] = low
    weights = (
        2.25 * inverse,
        inverse * square * (-0.75 - 0.5 * 3.375),
        inverse * square * square * (0.5 * 3.375),
        inverse * square * square * square * (-0.5 * 1.125),
        inverse * square * square * square * square * (0.5 * 0.125),
    )
    second = sum(w * p for w, p in zip(weights, powers))

    def applied(value):
        once = thin((x_hi, x_lo), *split(value))
        twice = thin((x_hi, x_lo), *split(once))
        return 1.5 * once - 0.5 * thin((x_hi, x_lo), *split(twice))

    third = 1.5 * second - 0.5 * applied(applied(second))
    for a in range(SLOTS):
        block = -third[a * B:a * B + B]
        if a == 0:
            block = jnp.where(eye, 1.0, 0.0) + block
        halves[a] = 0.5 * block
    share_out = Exchange(dhood, sends, recvs, COPIES, gx, gy, n_gx, n_gy, False)
    for code in range(9):
        slot = jnp.int32(0)
        held = codes[0] == code
        for a in range(1, SLOTS):
            slot = jnp.where(codes[a] == code, a, slot)
            held = held | (codes[a] == code)
        block = jnp.where(held, halves[slot], 0.0)
        dhood[4, code // 3, code % 3] = block.astype(BF16)
        density_ref[0, 0, code] = block
    for order in range(3):
        share_out.begin_row(order)
    share_out.begin_x()
    load_basis.wait()

    def tile(place, first):
        near_x, near_y = place // 3 - 1, place % 3 - 1
        lefts, rights = [], []
        for code in range(9):
            far_x, far_y = near_x + code // 3 - 1, near_y + code % 3 - 1
            if abs(far_x) <= 1 and abs(far_y) <= 1:
                lefts.append((far_x + 1) * 3 + far_y + 1)
                rights.append(dhood[place, code // 3, code % 3])
        right = jnp.concatenate(rights, axis=0)
        for start in range(0, grid_acc.shape[0], 256):
            rows = slice(start, start + 256)
            left = jnp.concatenate([basis[e, rows, :] for e in lefts], axis=1)
            product = jnp.dot(left, right, preferred_element_type=F32)
            product = product * basis[place, rows, :].astype(F32)
            if first:
                grid_acc[rows, :] = product
            else:
                grid_acc[rows, :] = grid_acc[rows, :] + product

    tile(4, True)
    share_out.forward(0)
    share_out.forward(1)
    share_out.wait_x()
    tile(BELOW_X, False)
    share_out.forward(2)
    tile(ABOVE_X, False)
    tile(BELOW_Y, False)
    tile(ABOVE_Y, False)
    share_out.wait_onward()
    for place in (0, 2, 6, 8):
        tile(place, False)
    for part in range(grid_acc.shape[0] // B):
        block = grid_acc[part * B:part * B + B, :].T
        grid_ref[:, part * B:part * B + B] = jnp.sum(block.reshape(B // 8, 8, B), axis=0)

    swap.wait_sent()
    share_out.wait_sent()
    for copy in along_x + along_y:
        copy.wait_send()


def local(n_gx, n_gy, hblocks, onsite, pattern, slot_code, basis):
    points = basis.shape[3]
    total = COPIES
    hbm = pl.BlockSpec(memory_space=pltpu.HBM)
    vmem = pl.BlockSpec(memory_space=pltpu.VMEM)
    square = (ORDER, ORDER)
    hblocks, onsite, pattern, slot_code, basis = [
        pltpu.with_memory_space_constraint(x, pltpu.HBM)
        for x in (hblocks, onsite, pattern, slot_code, basis)
    ]
    density, grid = pl.pallas_call(
        functools.partial(kernel, n_gx, n_gy),
        out_shape=(
            jax.ShapeDtypeStruct((1, 1, 9, B, B), F32),
            jax.ShapeDtypeStruct((8, points), F32),
        ),
        in_specs=[hbm] * 5,
        out_specs=(vmem, vmem),
        scratch_shapes=[
            pltpu.VMEM((9, B, B), F32),
            pltpu.VMEM((1, 1, B), F32),
            pltpu.SMEM((1, 1, 9), jnp.int32),
            pltpu.SMEM((1, 1, SLOTS), jnp.int32),
            pltpu.VMEM((9, points, B), BF16),
            pltpu.VMEM((9, 3, 6, B, B), BF16),
            pltpu.VMEM(square, F32),
            pltpu.VMEM(square, BF16),
            pltpu.VMEM(square, BF16),
            pltpu.VMEM(square, BF16),
            pltpu.VMEM(square, BF16),
            pltpu.VMEM(square, F32),
            pltpu.VMEM(square, BF16),
            pltpu.VMEM(square, BF16),
            pltpu.VMEM((SLOTS, B, B), F32),
            pltpu.VMEM((9, 3, 3, B, B), BF16),
            pltpu.VMEM((points, B), F32),
            pltpu.VMEM((2, 8, B), F32),
            pltpu.VMEM((n_gx - 1, 8, B), F32),
            pltpu.VMEM((n_gy - 1, 8, B), F32),
            pltpu.SemaphoreType.DMA((7,)),
            pltpu.SemaphoreType.DMA((2 * total,)),
            pltpu.SemaphoreType.DMA((2 * total,)),
            pltpu.SemaphoreType.DMA((n_gx - 1,)),
            pltpu.SemaphoreType.DMA((n_gx - 1,)),
            pltpu.SemaphoreType.DMA((n_gy - 1,)),
            pltpu.SemaphoreType.DMA((n_gy - 1,)),
        ],
        compiler_params=pltpu.CompilerParams(
            collective_id=0, has_side_effects=True, vmem_limit_bytes=40 << 20
        ),
    )(hblocks, onsite, pattern, slot_code, basis)
    return density.astype(BF16), jnp.sum(grid, axis=0)[None, None]


def solution(mesh):
    placed = (
        P("gx", "gy", None, None, None),
        P("gx", "gy", None),
        P("gx", "gy", None),
        P("gx", "gy", None),
        P("gx", "gy", None, None, None),
    )
    return jax.shard_map(
        functools.partial(local, mesh.shape["gx"], mesh.shape["gy"]),
        mesh=mesh,
        in_specs=placed,
        out_specs=(P("gx", "gy", None, None, None), P("gx", "gy", None)),
        check_vma=False,
    )
```

```python
import functools

import jax
import jax.numpy as jnp
from jax import lax
from jax.experimental import pallas as pl
from jax.experimental.pallas import tpu as pltpu
from jax.sharding import PartitionSpec as P

POWER_STEPS = 6
B = 128
SLOTS = 6
ORDER = SLOTS * B
MESH = pl.DeviceIdType.MESH
F32 = jnp.float32
BF16 = jnp.bfloat16

BELOW_X, ABOVE_X, BELOW_Y, ABOVE_Y = 1, 7, 3, 5
COPIES = 18 + 14 + 10

HIGH = 1
LOW = (0, 5, 4)


def split(value):
    high = value.astype(BF16)
    return high, (value - high.astype(F32)).astype(BF16)


class Exchange:
    def __init__(self, hood, sends, recvs, base, gx, gy, n_gx, n_gy, lows):
        odd = lax.rem(gx, 2)
        up_y = (gx, lax.rem(gy + 1, n_gy))
        down_y = (gx, lax.rem(gy + n_gy - 1, n_gy))
        step = 2 * odd - 1
        far = (lax.rem(gx + step + n_gx, n_gx), gy)
        near = (gx - step, gy)
        self.index = base

        def copy(source, target, rows, columns, device):
            index = self.index
            self.index += 1
            return pltpu.make_async_remote_copy(
                src_ref=hood.at[source, rows, columns],
                dst_ref=hood.at[target, rows, columns],
                send_sem=sends.at[index],
                recv_sem=recvs.at[index],
                device_id=device,
                device_id_type=MESH,
            )

        def planes(place, low):
            if not lows:
                return (1, 2) if place == BELOW_Y else (0, 1)
            if place == BELOW_Y:
                return (2, 3, 4) if low else (2, 3)
            return (1, 2, 0) if low else (1, 2)

        towards_far = pl.ds(2 * odd, 1)
        towards_near = pl.ds(2 - 2 * odd, 1)
        middle = pl.ds(1, 1)
        to_far, to_near = (far, -3 * step), (near, 3 * step)
        sides = ((BELOW_Y, up_y), (ABOVE_Y, down_y))
        self.steps = []

        def add(rows, targets, low, only_low=False):
            for which in range(3 if lows else 2):
                is_low = which == 2
                if is_low and not low or only_low and not is_low:
                    continue
                for place, device in sides:
                    plane = planes(place, True)[which]
                    columns = slice(plane, plane + 1)
                    arriving = copy(4, place, rows, columns, device)
                    going = [copy(place, place + shift, rows, columns, peer) for peer, shift in targets]
                    self.steps.append((arriving, going))

        add(middle, (to_far, to_near), False)
        add(towards_far, (to_far,), lows)
        add(towards_near, (to_near,), lows)
        if lows:
            add(middle, (), True, True)
        across = slice(1, 4) if lows else slice(0, 3)
        self.along_x = [
            copy(4, 4 - 3 * step, pl.ds(odd, 2), across, far),
            copy(4, 4 + 3 * step, pl.ds(1 - odd, 2), across, near),
        ]
        if lows:
            single = slice(LOW[1], LOW[1] + 1)
            self.along_x += [
                copy(4, 4 - 3 * step, towards_far, single, far),
                copy(4, 4 + 3 * step, towards_near, single, near),
            ]
        self.to_far = [c for n, (_, copies) in enumerate(self.steps) for c in copies[:1] if n < (10 if lows else 8)]
        self.to_near = [c for n, (_, copies) in enumerate(self.steps) for c in copies[-1:] if n < 4 or n >= (10 if lows else 8)]

    def begin(self, first, last):
        for arriving, _ in self.steps[first:last]:
            arriving.start()

    def begin_x(self):
        for copy in self.along_x:
            copy.start()

    def forward(self, first, last):
        for arriving, going in self.steps[first:last]:
            arriving.wait_recv()
            for copy in going:
                copy.start()

    def wait(self, copies):
        for copy in copies:
            copy.wait_recv()

    def wait_sent(self):
        for arriving, going in self.steps:
            arriving.wait_send()
            for copy in going:
                copy.wait_send()
        for copy in self.along_x:
            copy.wait_send()


def three(left, right):
    lhs = jnp.concatenate([left[0], left[0], left[1]], axis=1)
    rhs = jnp.concatenate([right[0], right[1], right[0]], axis=0)
    return jnp.dot(lhs, rhs, preferred_element_type=F32)


def thin(matrix, high, low):
    rhs = jnp.concatenate([high, low], axis=1)
    out = []
    for start in range(0, ORDER, 256):
        rows = slice(start, start + 256)
        both = jnp.dot(matrix[0][rows, :], rhs, preferred_element_type=F32)
        rest = jnp.dot(matrix[1][rows, :], high, preferred_element_type=F32)
        out.append(both[:, :B] + (both[:, B:] + rest))
    return jnp.concatenate(out, axis=0)


def kernel(
    n_gx, n_gy,
    h_any, onsite_any, pattern_any, code_any, basis_any,
    density_ref, grid_ref,
    h_buf, onsite_ref, pattern_ref, code_ref, basis, hood, m_f, m_hi, m_lo, q_hi, q_lo, n_f, x_hi, x_lo,
    halves, dhood, grid_acc, best, best_x, best_y,
    in_sem, sends, recvs, sends_x, recvs_x, sends_y, recvs_y,
):
    gx, gy = lax.axis_index("gx"), lax.axis_index("gy")

    barrier = pltpu.get_barrier_semaphore()
    for step in range(1, n_gx):
        pl.semaphore_signal(barrier, inc=1, device_id=(lax.rem(gx + step, n_gx), gy), device_id_type=MESH)
    for step in range(1, n_gy):
        pl.semaphore_signal(barrier, inc=1, device_id=(gx, lax.rem(gy + step, n_gy)), device_id_type=MESH)
    loads = []
    for order, row in enumerate((1, 0, 2)):
        rows = pl.ds(3 * row, 3)
        loads.append(pltpu.make_async_copy(h_any.at[0, 0, rows], h_buf.at[rows], in_sem.at[order]))
        loads[-1].start()
        if order == 0:
            load_pattern = pltpu.make_async_copy(pattern_any, pattern_ref, in_sem.at[4])
            load_onsite = pltpu.make_async_copy(onsite_any, onsite_ref, in_sem.at[5])
            load_codes = pltpu.make_async_copy(code_any, code_ref, in_sem.at[6])
            load_pattern.start()
            load_onsite.start()
            load_codes.start()
    load_basis = pltpu.make_async_copy(basis_any.at[0, 0], basis, in_sem.at[3])
    load_basis.start()

    rows_of = lax.broadcasted_iota(jnp.int32, (B, B), 0)
    columns_of = lax.broadcasted_iota(jnp.int32, (B, B), 1)
    eye = rows_of == columns_of

    def prepare(row):
        for col in range(3):
            code = 3 * row + col
            block = h_buf[code]
            if code == 4:
                block = block + jnp.where(eye, onsite_ref[0], 0.0)
            else:
                block = block * pattern_ref[0, 0, code].astype(F32)
            high, low = split(block)
            hood[4, row, HIGH + col] = high
            hood[4, row, LOW[col]] = low

    swap = Exchange(hood, sends, recvs, 0, gx, gy, n_gx, n_gy, True)
    load_pattern.wait()
    load_onsite.wait()
    load_codes.wait()
    loads[0].wait()
    prepare(1)
    pl.semaphore_wait(barrier, n_gx + n_gy - 2)
    swap.begin(0, 4)
    loads[1].wait()
    prepare(0)
    loads[2].wait()
    prepare(2)
    swap.begin(4, 18)
    swap.begin_x()
    swap.forward(0, 18)
    swap.wait(swap.along_x + swap.to_near + swap.to_far)

    codes = [code_ref[0, 0, a] for a in range(SLOTS)]
    used = [code < 9 for code in codes]
    safe = [jnp.where(u, code, 4) for u, code in zip(used, codes)]
    off_x = [lax.div(s, 3) - 1 for s in safe]
    off_y = [lax.rem(s, 3) - 1 for s in safe]

    def stored(a, b):
        dx, dy = off_x[a] - off_x[b], off_y[a] - off_y[b]
        valid = (jnp.abs(dx) <= 1) & (jnp.abs(dy) <= 1) & used[a] & used[b]
        source = jnp.where(valid, safe[b], 4)
        row = jnp.where(valid, dx + 1, 1)
        col = jnp.where(valid, dy + 1, 1)
        block = hood[source, row, col + HIGH].astype(F32)
        if a == 0 or b == 0:
            plane = jnp.where(col == 1, LOW[1], jnp.where(col == 0, LOW[0], LOW[2]))
            block = block + hood[source, row, plane].astype(F32)
        return jnp.where(valid, block, 0.0)

    def put(a, b, block):
        place = (slice(a * B, a * B + B), slice(b * B, b * B + B))
        m_f[place] = block
        high, low = split(block)
        m_hi[place] = high
        m_lo[place] = low

    for a in range(SLOTS):
        block = stored(a, a)
        put(a, a, 0.5 * (block + block.T))
        for b in range(a + 1, SLOTS):
            upper = 0.5 * (stored(a, b) + stored(b, a).T)
            put(a, b, upper)
            put(b, a, upper.T)

    def from_rows(vector):
        out = []
        for b in range(SLOTS):
            total = jnp.zeros((8, B), F32)
            for a in range(SLOTS):
                part = m_f[a * B:a * B + B, b * B:b * B + B] * vector[a]
                total = total + jnp.sum(part.reshape(B // 8, 8, B), axis=0)
            out.append(jnp.sum(total, axis=0, keepdims=True))
        return out

    def from_lanes(vector):
        out = []
        for a in range(SLOTS):
            total = jnp.zeros((B, B), F32)
            for b in range(SLOTS):
                total = total + m_f[a * B:a * B + B, b * B:b * B + B] * vector[b]
            out.append(jnp.sum(total, axis=1, keepdims=True))
        return out

    def norm2(vector):
        total = sum(part * part for part in vector)
        return jnp.sum(total, keepdims=True) + 1e-6

    vector = [jnp.full((B, 1), 1.0, F32) * u.astype(F32) for u in used]
    for step in range(POWER_STEPS + 1):
        image = from_rows(vector) if step % 2 == 0 else from_lanes(vector)
        squares = norm2(image)
        if step < POWER_STEPS:
            factor = lax.rsqrt(squares)
            vector = [part * factor for part in image]
    estimate = jnp.sqrt(squares)
    best[0] = jnp.broadcast_to(estimate, (8, B))

    def share(source, target, sends_to, recvs_to, count, axis):
        out = []
        for step in range(1, count):
            peer = (lax.rem(gx + step, n_gx), gy) if axis == 0 else (gx, lax.rem(gy + step, n_gy))
            out.append(pltpu.make_async_remote_copy(
                src_ref=best.at[source],
                dst_ref=target.at[step - 1],
                send_sem=sends_to.at[step - 1],
                recv_sem=recvs_to.at[step - 1],
                device_id=peer,
                device_id_type=MESH,
            ))
        return out

    along_x = share(0, best_x, sends_x, recvs_x, n_gx, 0)
    along_y = share(1, best_y, sends_y, recvs_y, n_gy, 1)
    for copy in along_x:
        copy.start()

    for r in range(0, ORDER, 256):
        for c in range(r, ORDER, 256):
            rows, cols = slice(r, r + 256), slice(c, c + 256)
            block = three((m_hi[rows, :], m_lo[rows, :]), (m_hi[:, cols], m_lo[:, cols]))
            high, low = split(block)
            q_hi[rows, cols] = high
            q_lo[rows, cols] = low
            if r != c:
                high, low = split(block.T)
                q_hi[cols, rows] = high
                q_lo[cols, rows] = low

    top = best[0]
    for step, copy in enumerate(along_x):
        copy.wait_recv()
        top = jnp.maximum(top, best_x[step])
    best[1] = top
    for copy in along_y:
        copy.start()

    for r in range(0, ORDER, 256):
        for c in range(r, ORDER, 256):
            rows, cols = slice(r, r + 256), slice(c, c + 256)
            block = three((m_hi[rows, :], m_lo[rows, :]), (q_hi[:, cols], q_lo[:, cols]))
            n_f[rows, cols] = block
            if r != c:
                n_f[cols, rows] = block.T

    powers = [m_f[:, :B], n_f[:, :B]]
    for _ in range(3):
        powers.append(thin((q_hi, q_lo), *split(powers[-1])))

    top = best[1]
    for step, copy in enumerate(along_y):
        copy.wait_recv()
        top = jnp.maximum(top, best_y[step])
    inverse = 1.0 / (1.25 * top[:1, :1])
    square = inverse * inverse

    alpha, beta = 1.5 * inverse, -0.5 * inverse * square
    for r in range(0, ORDER, B):
        rows = slice(r, r + B)
        high, low = split(alpha * m_f[rows, :] + beta * n_f[rows, :])
        x_hi[rows, :] = high
        x_lo[rows, :] = low
    weights = (
        2.25 * inverse,
        inverse * square * (-0.75 - 0.5 * 3.375),
        inverse * square * square * (0.5 * 3.375),
        inverse * square * square * square * (-0.5 * 1.125),
        inverse * square * square * square * square * (0.5 * 0.125),
    )
    second = sum(w * p for w, p in zip(weights, powers))

    def applied(value):
        once = thin((x_hi, x_lo), *split(value))
        twice = thin((x_hi, x_lo), *split(once))
        return 1.5 * once - 0.5 * thin((x_hi, x_lo), *split(twice))

    third = 1.5 * second - 0.5 * applied(applied(second))
    for a in range(SLOTS):
        block = -third[a * B:a * B + B]
        if a == 0:
            block = jnp.where(eye, 1.0, 0.0) + block
        halves[a] = 0.5 * block
    share_out = Exchange(dhood, sends, recvs, COPIES, gx, gy, n_gx, n_gy, False)
    for code in range(9):
        slot = jnp.int32(0)
        held = codes[0] == code
        for a in range(1, SLOTS):
            slot = jnp.where(codes[a] == code, a, slot)
            held = held | (codes[a] == code)
        block = jnp.where(held, halves[slot], 0.0).astype(BF16)
        dhood[4, code // 3, code % 3] = block
        density_ref[0, 0, code] = block
    share_out.begin(0, 12)
    share_out.begin_x()
    load_basis.wait()

    step = 2 * lax.rem(gx, 2) - 1

    def tile(near_x, near_y, first=False):
        fixed = isinstance(near_x, int)
        place = (near_x + 1) * 3 + near_y + 1
        if fixed:
            firsts = range(max(-near_x, 0), 3 - max(near_x, 0))
        else:
            start = lax.div(1 - near_x, 2)
            firsts = (start, start + 1)
        lefts, rights = [], []
        for row in firsts:
            for col in range(3):
                far_y = near_y + col - 1
                if abs(far_y) <= 1:
                    lefts.append((near_x + row) * 3 + far_y + 1)
                    rights.append(dhood[place, row, col])
        right = jnp.concatenate(rights, axis=0)
        for start in range(0, grid_acc.shape[0], 256):
            rows = slice(start, start + 256)
            left = jnp.concatenate([basis[e, rows, :] for e in lefts], axis=1)
            product = jnp.dot(left, right, preferred_element_type=F32)
            product = product * basis[place, rows, :].astype(F32)
            if first:
                grid_acc[rows, :] = product
            else:
                grid_acc[rows, :] = grid_acc[rows, :] + product

    tile(0, 0, True)
    share_out.forward(0, 8)
    share_out.wait(share_out.along_x)
    tile(-1, 0)
    share_out.forward(8, 12)
    tile(1, 0)
    tile(0, -1)
    tile(0, 1)
    share_out.wait(share_out.to_near)
    tile(-step, -1)
    tile(-step, 1)
    share_out.wait(share_out.to_far)
    tile(step, -1)
    tile(step, 1)
    for part in range(grid_acc.shape[0] // B):
        block = grid_acc[part * B:part * B + B, :].T
        grid_ref[0, :, pl.ds(part * B, B)] = jnp.sum(block, axis=0, keepdims=True)

    swap.wait_sent()
    share_out.wait_sent()
    for copy in along_x + along_y:
        copy.wait_send()


def write_out(density_in, grid_in, density_out, grid_out, sems):
    first = pltpu.make_async_copy(density_in, density_out, sems.at[0])
    second = pltpu.make_async_copy(grid_in, grid_out, sems.at[1])
    first.start()
    second.start()
    first.wait()
    second.wait()


def local(n_gx, n_gy, hblocks, onsite, pattern, slot_code, basis):
    points = basis.shape[3]
    total = COPIES
    hbm = pl.BlockSpec(memory_space=pltpu.HBM)
    vmem = pl.BlockSpec(memory_space=pltpu.VMEM)
    square = (ORDER, ORDER)
    hblocks, onsite, pattern, slot_code, basis = [
        pltpu.with_memory_space_constraint(x, pltpu.HBM)
        for x in (hblocks, onsite, pattern, slot_code, basis)
    ]
    density, grid = pl.pallas_call(
        functools.partial(kernel, n_gx, n_gy),
        out_shape=(
            jax.ShapeDtypeStruct((1, 1, 9, B, B), BF16),
            jax.ShapeDtypeStruct((1, 1, points), F32),
        ),
        in_specs=[hbm] * 5,
        out_specs=(vmem, vmem),
        scratch_shapes=[
            pltpu.VMEM((9, B, B), F32),
            pltpu.VMEM((1, 1, B), F32),
            pltpu.SMEM((1, 1, 9), jnp.int32),
            pltpu.SMEM((1, 1, SLOTS), jnp.int32),
            pltpu.VMEM((9, points, B), BF16),
            pltpu.VMEM((9, 3, 6, B, B), BF16),
            pltpu.VMEM(square, F32),
            pltpu.VMEM(square, BF16),
            pltpu.VMEM(square, BF16),
            pltpu.VMEM(square, BF16),
            pltpu.VMEM(square, BF16),
            pltpu.VMEM(square, F32),
            pltpu.VMEM(square, BF16),
            pltpu.VMEM(square, BF16),
            pltpu.VMEM((SLOTS, B, B), F32),
            pltpu.VMEM((9, 3, 3, B, B), BF16),
            pltpu.VMEM((points, B), F32),
            pltpu.VMEM((2, 8, B), F32),
            pltpu.VMEM((n_gx - 1, 8, B), F32),
            pltpu.VMEM((n_gy - 1, 8, B), F32),
            pltpu.SemaphoreType.DMA((7,)),
            pltpu.SemaphoreType.DMA((2 * total,)),
            pltpu.SemaphoreType.DMA((2 * total,)),
            pltpu.SemaphoreType.DMA((n_gx - 1,)),
            pltpu.SemaphoreType.DMA((n_gx - 1,)),
            pltpu.SemaphoreType.DMA((n_gy - 1,)),
            pltpu.SemaphoreType.DMA((n_gy - 1,)),
        ],
        compiler_params=pltpu.CompilerParams(
            collective_id=0, has_side_effects=True, vmem_limit_bytes=40 << 20
        ),
    )(hblocks, onsite, pattern, slot_code, basis)
    space = pl.BlockSpec(memory_space=pl.ANY)
    return pl.pallas_call(
        write_out,
        out_shape=(
            jax.ShapeDtypeStruct(density.shape, BF16),
            jax.ShapeDtypeStruct(grid.shape, F32),
        ),
        in_specs=[vmem, vmem],
        out_specs=(space, space),
        scratch_shapes=[pltpu.SemaphoreType.DMA((2,))],
    )(*[pltpu.with_memory_space_constraint(x, pltpu.VMEM) for x in (density, grid)])


def solution(mesh):
    placed = (
        P("gx", "gy", None, None, None),
        P("gx", "gy", None),
        P("gx", "gy", None),
        P("gx", "gy", None),
        P("gx", "gy", None, None, None),
    )
    return jax.shard_map(
        functools.partial(local, mesh.shape["gx"], mesh.shape["gy"]),
        mesh=mesh,
        in_specs=placed,
        out_specs=(P("gx", "gy", None, None, None), P("gx", "gy", None)),
        check_vma=False,
    )
```

```python
import functools

import jax
import jax.numpy as jnp
from jax import lax
from jax.experimental import pallas as pl
from jax.experimental.pallas import tpu as pltpu
from jax.sharding import PartitionSpec as P

POWER_STEPS = 6
B = 128
SLOTS = 6
ORDER = SLOTS * B
MESH = pl.DeviceIdType.MESH
F32 = jnp.float32
BF16 = jnp.bfloat16

BELOW_X, ABOVE_X, BELOW_Y, ABOVE_Y = 1, 7, 3, 5
COPIES = 18 + 14 + 10

HIGH = 1
LOW = (0, 5, 4)


def split(value):
    high = value.astype(BF16)
    return high, (value - high.astype(F32)).astype(BF16)


class Exchange:
    def __init__(self, hood, sends, recvs, base, gx, gy, n_gx, n_gy, lows):
        odd = lax.rem(gx, 2)
        up_y = (gx, lax.rem(gy + 1, n_gy))
        down_y = (gx, lax.rem(gy + n_gy - 1, n_gy))
        step = 2 * odd - 1
        far = (lax.rem(gx + step + n_gx, n_gx), gy)
        near = (gx - step, gy)
        self.index = base

        def copy(source, target, rows, columns, device):
            index = self.index
            self.index += 1
            return pltpu.make_async_remote_copy(
                src_ref=hood.at[source, rows, columns],
                dst_ref=hood.at[target, rows, columns],
                send_sem=sends.at[index],
                recv_sem=recvs.at[index],
                device_id=device,
                device_id_type=MESH,
            )

        def planes(place, low):
            if not lows:
                return (1, 2) if place == BELOW_Y else (0, 1)
            if place == BELOW_Y:
                return (2, 3, 4) if low else (2, 3)
            return (1, 2, 0) if low else (1, 2)

        towards_far = pl.ds(2 * odd, 1)
        towards_near = pl.ds(2 - 2 * odd, 1)
        middle = pl.ds(1, 1)
        to_far, to_near = (far, -3 * step), (near, 3 * step)
        sides = ((BELOW_Y, up_y), (ABOVE_Y, down_y))
        self.steps = []

        def add(rows, targets, low, only_low=False):
            for which in range(3 if lows else 2):
                is_low = which == 2
                if is_low and not low or only_low and not is_low:
                    continue
                for place, device in sides:
                    plane = planes(place, True)[which]
                    columns = slice(plane, plane + 1)
                    arriving = copy(4, place, rows, columns, device)
                    going = [copy(place, place + shift, rows, columns, peer) for peer, shift in targets]
                    self.steps.append((arriving, going))

        add(middle, (to_far, to_near), False)
        add(towards_far, (to_far,), lows)
        add(towards_near, (to_near,), lows)
        if lows:
            add(middle, (), True, True)
        across = slice(1, 4) if lows else slice(0, 3)
        self.along_x = [
            copy(4, 4 - 3 * step, pl.ds(odd, 2), across, far),
            copy(4, 4 + 3 * step, pl.ds(1 - odd, 2), across, near),
        ]
        if lows:
            single = slice(LOW[1], LOW[1] + 1)
            self.along_x += [
                copy(4, 4 - 3 * step, towards_far, single, far),
                copy(4, 4 + 3 * step, towards_near, single, near),
            ]
        self.to_far = [c for n, (_, copies) in enumerate(self.steps) for c in copies[:1] if n < (10 if lows else 8)]
        self.to_near = [c for n, (_, copies) in enumerate(self.steps) for c in copies[-1:] if n < 4 or n >= (10 if lows else 8)]

    def begin(self, first, last):
        for arriving, _ in self.steps[first:last]:
            arriving.start()

    def begin_x(self):
        for copy in self.along_x:
            copy.start()

    def forward(self, first, last):
        for arriving, going in self.steps[first:last]:
            arriving.wait_recv()
            for copy in going:
                copy.start()

    def wait(self, copies):
        for copy in copies:
            copy.wait_recv()

    def wait_sent(self):
        for arriving, going in self.steps:
            arriving.wait_send()
            for copy in going:
                copy.wait_send()
        for copy in self.along_x:
            copy.wait_send()


def three(left, right):
    lhs = jnp.concatenate([left[0], left[0], left[1]], axis=1)
    rhs = jnp.concatenate([right[0], right[1], right[0]], axis=0)
    return jnp.dot(lhs, rhs, preferred_element_type=F32)


def thin(matrix, high, low):
    rhs = jnp.concatenate([high, low], axis=1)
    out = []
    for start in range(0, ORDER, 256):
        rows = slice(start, start + 256)
        both = jnp.dot(matrix[0][rows, :], rhs, preferred_element_type=F32)
        rest = jnp.dot(matrix[1][rows, :], high, preferred_element_type=F32)
        out.append(both[:, :B] + (both[:, B:] + rest))
    return jnp.concatenate(out, axis=0)


def kernel(
    n_gx, n_gy,
    h_any, onsite_any, pattern_any, code_any, basis_any,
    density_ref, grid_ref,
    h_buf, onsite_ref, pattern_ref, code_ref, basis, hood, m_f, m_hi, m_lo, q_hi, q_lo, n_f, x_hi, x_lo,
    halves, dhood, grid_acc, best, best_x, best_y,
    in_sem, sends, recvs, sends_x, recvs_x, sends_y, recvs_y,
):
    gx, gy = lax.axis_index("gx"), lax.axis_index("gy")

    small = [
        pltpu.make_async_copy(source, target, in_sem.at[4 + n])
        for n, (source, target) in enumerate((
            (pattern_any, pattern_ref), (onsite_any, onsite_ref), (code_any, code_ref),
        ))
    ]
    loads = []
    for order, row in enumerate((1, 0, 2)):
        rows = pl.ds(3 * row, 3)
        loads.append(pltpu.make_async_copy(h_any.at[0, 0, rows], h_buf.at[rows], in_sem.at[order]))
    for copy in [loads[0]] + small:
        copy.start()
    barrier = pltpu.get_barrier_semaphore()
    for step in range(1, n_gx):
        pl.semaphore_signal(barrier, inc=1, device_id=(lax.rem(gx + step, n_gx), gy), device_id_type=MESH)
    for step in range(1, n_gy):
        pl.semaphore_signal(barrier, inc=1, device_id=(gx, lax.rem(gy + step, n_gy)), device_id_type=MESH)
    loads[1].start()
    loads[2].start()
    load_basis = pltpu.make_async_copy(basis_any.at[0, 0], basis, in_sem.at[3])
    load_basis.start()

    rows_of = lax.broadcasted_iota(jnp.int32, (B, B), 0)
    columns_of = lax.broadcasted_iota(jnp.int32, (B, B), 1)
    eye = rows_of == columns_of

    def prepare(row):
        for col in range(3):
            code = 3 * row + col
            block = h_buf[code]
            if code == 4:
                block = block + jnp.where(eye, onsite_ref[0], 0.0)
            else:
                block = block * pattern_ref[0, 0, code].astype(F32)
            high, low = split(block)
            hood[4, row, HIGH + col] = high
            hood[4, row, LOW[col]] = low

    swap = Exchange(hood, sends, recvs, 0, gx, gy, n_gx, n_gy, True)
    for copy in small + [loads[0]]:
        copy.wait()
    prepare(1)
    pl.semaphore_wait(barrier, n_gx + n_gy - 2)
    swap.begin(0, 4)
    loads[1].wait()
    prepare(0)
    loads[2].wait()
    prepare(2)
    swap.begin(4, 18)
    swap.begin_x()
    swap.forward(0, 18)
    swap.wait(swap.along_x + swap.to_near + swap.to_far)

    codes = [code_ref[0, 0, a] for a in range(SLOTS)]
    used = [code < 9 for code in codes]
    safe = [jnp.where(u, code, 4) for u, code in zip(used, codes)]
    off_x = [lax.div(s, 3) - 1 for s in safe]
    off_y = [lax.rem(s, 3) - 1 for s in safe]

    def stored(a, b):
        dx, dy = off_x[a] - off_x[b], off_y[a] - off_y[b]
        valid = (jnp.abs(dx) <= 1) & (jnp.abs(dy) <= 1) & used[a] & used[b]
        source = jnp.where(valid, safe[b], 4)
        row = jnp.where(valid, dx + 1, 1)
        col = jnp.where(valid, dy + 1, 1)
        block = hood[source, row, col + HIGH].astype(F32)
        if a == 0 or b == 0:
            plane = jnp.where(col == 1, LOW[1], jnp.where(col == 0, LOW[0], LOW[2]))
            block = block + hood[source, row, plane].astype(F32)
        return jnp.where(valid, block, 0.0)

    def put(a, b, block):
        place = (slice(a * B, a * B + B), slice(b * B, b * B + B))
        m_f[place] = block
        high, low = split(block)
        m_hi[place] = high
        m_lo[place] = low

    for a in range(SLOTS):
        block = stored(a, a)
        put(a, a, 0.5 * (block + block.T))
        for b in range(a + 1, SLOTS):
            upper = 0.5 * (stored(a, b) + stored(b, a).T)
            put(a, b, upper)
            put(b, a, upper.T)

    def from_rows(vector):
        out = []
        for b in range(SLOTS):
            total = jnp.zeros((8, B), F32)
            for a in range(SLOTS):
                part = m_f[a * B:a * B + B, b * B:b * B + B] * vector[a]
                total = total + jnp.sum(part.reshape(B // 8, 8, B), axis=0)
            out.append(jnp.sum(total, axis=0, keepdims=True))
        return out

    def from_lanes(vector):
        out = []
        for a in range(SLOTS):
            total = jnp.zeros((B, B), F32)
            for b in range(SLOTS):
                total = total + m_f[a * B:a * B + B, b * B:b * B + B] * vector[b]
            out.append(jnp.sum(total, axis=1, keepdims=True))
        return out

    def norm2(vector):
        total = sum(part * part for part in vector)
        return jnp.sum(total, keepdims=True)

    vector = [jnp.full((B, 1), 1.0, F32) * u.astype(F32) for u in used]
    length = jnp.ones((1, 1), F32)
    for step in range(POWER_STEPS + 1):
        image = from_rows(vector) if step % 2 == 0 else from_lanes(vector)
        total = norm2(image)
        factor = 1.0 / length
        if step < POWER_STEPS:
            vector = [part * factor for part in image]
            length = factor * jnp.sqrt(total + 1e-6 * (length * length))
    estimate = jnp.sqrt(total * (factor * factor) + 1e-6)
    best[0] = jnp.broadcast_to(estimate, (8, B))

    def share(source, target, sends_to, recvs_to, count, axis):
        out = []
        for step in range(1, count):
            peer = (lax.rem(gx + step, n_gx), gy) if axis == 0 else (gx, lax.rem(gy + step, n_gy))
            out.append(pltpu.make_async_remote_copy(
                src_ref=best.at[source],
                dst_ref=target.at[step - 1],
                send_sem=sends_to.at[step - 1],
                recv_sem=recvs_to.at[step - 1],
                device_id=peer,
                device_id_type=MESH,
            ))
        return out

    along_x = share(0, best_x, sends_x, recvs_x, n_gx, 0)
    along_y = share(1, best_y, sends_y, recvs_y, n_gy, 1)
    for copy in along_x:
        copy.start()

    for r in range(0, ORDER, 256):
        for c in range(r, ORDER, 256):
            rows, cols = slice(r, r + 256), slice(c, c + 256)
            block = three((m_hi[rows, :], m_lo[rows, :]), (m_hi[:, cols], m_lo[:, cols]))
            high, low = split(block)
            q_hi[rows, cols] = high
            q_lo[rows, cols] = low
            if r != c:
                high, low = split(block.T)
                q_hi[cols, rows] = high
                q_lo[cols, rows] = low

    top = best[0]
    for step, copy in enumerate(along_x):
        copy.wait_recv()
        top = jnp.maximum(top, best_x[step])
    best[1] = top
    for copy in along_y:
        copy.start()

    for r in range(0, ORDER, 256):
        for c in range(r, ORDER, 256):
            rows, cols = slice(r, r + 256), slice(c, c + 256)
            block = three((m_hi[rows, :], m_lo[rows, :]), (q_hi[:, cols], q_lo[:, cols]))
            n_f[rows, cols] = block
            if r != c:
                n_f[cols, rows] = block.T

    powers = [m_f[:, :B], n_f[:, :B]]
    for _ in range(3):
        powers.append(thin((q_hi, q_lo), *split(powers[-1])))

    top = best[1]
    for step, copy in enumerate(along_y):
        copy.wait_recv()
        top = jnp.maximum(top, best_y[step])
    inverse = 1.0 / (1.25 * top[:1, :1])
    square = inverse * inverse

    alpha, beta = 1.5 * inverse, -0.5 * inverse * square
    for r in range(0, ORDER, B):
        rows = slice(r, r + B)
        high, low = split(alpha * m_f[rows, :] + beta * n_f[rows, :])
        x_hi[rows, :] = high
        x_lo[rows, :] = low
    weights = (
        2.25 * inverse,
        inverse * square * (-0.75 - 0.5 * 3.375),
        inverse * square * square * (0.5 * 3.375),
        inverse * square * square * square * (-0.5 * 1.125),
        inverse * square * square * square * square * (0.5 * 0.125),
    )
    second = sum(w * p for w, p in zip(weights, powers))

    def applied(value):
        once = thin((x_hi, x_lo), *split(value))
        twice = thin((x_hi, x_lo), *split(once))
        return 1.5 * once - 0.5 * thin((x_hi, x_lo), *split(twice))

    third = 1.5 * second - 0.5 * applied(applied(second))
    for a in range(SLOTS):
        block = -third[a * B:a * B + B]
        if a == 0:
            block = jnp.where(eye, 1.0, 0.0) + block
        halves[a] = 0.5 * block
    share_out = Exchange(dhood, sends, recvs, COPIES, gx, gy, n_gx, n_gy, False)
    for code in range(9):
        slot = jnp.int32(0)
        held = codes[0] == code
        for a in range(1, SLOTS):
            slot = jnp.where(codes[a] == code, a, slot)
            held = held | (codes[a] == code)
        block = jnp.where(held, halves[slot], 0.0).astype(BF16)
        dhood[4, code // 3, code % 3] = block
        density_ref[0, 0, code] = block
    share_out.begin(0, 12)
    share_out.begin_x()
    load_basis.wait()

    step = 2 * lax.rem(gx, 2) - 1

    def tile(near_x, near_y, first=False):
        fixed = isinstance(near_x, int)
        place = (near_x + 1) * 3 + near_y + 1
        if fixed:
            firsts = range(max(-near_x, 0), 3 - max(near_x, 0))
        else:
            start = lax.div(1 - near_x, 2)
            firsts = (start, start + 1)
        lefts, rights = [], []
        for row in firsts:
            for col in range(3):
                far_y = near_y + col - 1
                if abs(far_y) <= 1:
                    lefts.append((near_x + row) * 3 + far_y + 1)
                    rights.append(dhood[place, row, col])
        right = jnp.concatenate(rights, axis=0)
        for start in range(0, grid_acc.shape[0], 256):
            rows = slice(start, start + 256)
            left = jnp.concatenate([basis[e, rows, :] for e in lefts], axis=1)
            product = jnp.dot(left, right, preferred_element_type=F32)
            product = product * basis[place, rows, :].astype(F32)
            if first:
                grid_acc[rows, :] = product
            else:
                grid_acc[rows, :] = grid_acc[rows, :] + product

    tile(0, 0, True)
    share_out.forward(0, 8)
    share_out.wait(share_out.along_x)
    tile(-1, 0)
    share_out.forward(8, 12)
    tile(1, 0)
    tile(0, -1)
    tile(0, 1)
    share_out.wait(share_out.to_near)
    tile(-step, -1)
    tile(-step, 1)
    share_out.wait(share_out.to_far)
    tile(step, -1)
    tile(step, 1)
    for part in range(grid_acc.shape[0] // B):
        block = grid_acc[part * B:part * B + B, :].T
        grid_ref[0, :, pl.ds(part * B, B)] = jnp.sum(block, axis=0, keepdims=True)

    swap.wait_sent()
    share_out.wait_sent()
    for copy in along_x + along_y:
        copy.wait_send()


def write_out(density_in, grid_in, density_out, grid_out, sems):
    first = pltpu.make_async_copy(density_in, density_out, sems.at[0])
    second = pltpu.make_async_copy(grid_in, grid_out, sems.at[1])
    first.start()
    second.start()
    first.wait()
    second.wait()


def local(n_gx, n_gy, hblocks, onsite, pattern, slot_code, basis):
    points = basis.shape[3]
    total = COPIES
    hbm = pl.BlockSpec(memory_space=pltpu.HBM)
    vmem = pl.BlockSpec(memory_space=pltpu.VMEM)
    square = (ORDER, ORDER)
    hblocks, onsite, pattern, slot_code, basis = [
        pltpu.with_memory_space_constraint(x, pltpu.HBM)
        for x in (hblocks, onsite, pattern, slot_code, basis)
    ]
    density, grid = pl.pallas_call(
        functools.partial(kernel, n_gx, n_gy),
        out_shape=(
            jax.ShapeDtypeStruct((1, 1, 9, B, B), BF16),
            jax.ShapeDtypeStruct((1, 1, points), F32),
        ),
        in_specs=[hbm] * 5,
        out_specs=(vmem, vmem),
        scratch_shapes=[
            pltpu.VMEM((9, B, B), F32),
            pltpu.VMEM((1, 1, B), F32),
            pltpu.SMEM((1, 1, 9), jnp.int32),
            pltpu.SMEM((1, 1, SLOTS), jnp.int32),
            pltpu.VMEM((9, points, B), BF16),
            pltpu.VMEM((9, 3, 6, B, B), BF16),
            pltpu.VMEM(square, F32),
            pltpu.VMEM(square, BF16),
            pltpu.VMEM(square, BF16),
            pltpu.VMEM(square, BF16),
            pltpu.VMEM(square, BF16),
            pltpu.VMEM(square, F32),
            pltpu.VMEM(square, BF16),
            pltpu.VMEM(square, BF16),
            pltpu.VMEM((SLOTS, B, B), F32),
            pltpu.VMEM((9, 3, 3, B, B), BF16),
            pltpu.VMEM((points, B), F32),
            pltpu.VMEM((2, 8, B), F32),
            pltpu.VMEM((n_gx - 1, 8, B), F32),
            pltpu.VMEM((n_gy - 1, 8, B), F32),
            pltpu.SemaphoreType.DMA((7,)),
            pltpu.SemaphoreType.DMA((2 * total,)),
            pltpu.SemaphoreType.DMA((2 * total,)),
            pltpu.SemaphoreType.DMA((n_gx - 1,)),
            pltpu.SemaphoreType.DMA((n_gx - 1,)),
            pltpu.SemaphoreType.DMA((n_gy - 1,)),
            pltpu.SemaphoreType.DMA((n_gy - 1,)),
        ],
        compiler_params=pltpu.CompilerParams(
            collective_id=0, has_side_effects=True, vmem_limit_bytes=40 << 20
        ),
    )(hblocks, onsite, pattern, slot_code, basis)
    space = pl.BlockSpec(memory_space=pl.ANY)
    return pl.pallas_call(
        write_out,
        out_shape=(
            jax.ShapeDtypeStruct(density.shape, BF16),
            jax.ShapeDtypeStruct(grid.shape, F32),
        ),
        in_specs=[vmem, vmem],
        out_specs=(space, space),
        scratch_shapes=[pltpu.SemaphoreType.DMA((2,))],
    )(*[pltpu.with_memory_space_constraint(x, pltpu.VMEM) for x in (density, grid)])


def solution(mesh):
    placed = (
        P("gx", "gy", None, None, None),
        P("gx", "gy", None),
        P("gx", "gy", None),
        P("gx", "gy", None),
        P("gx", "gy", None, None, None),
    )
    return jax.shard_map(
        functools.partial(local, mesh.shape["gx"], mesh.shape["gy"]),
        mesh=mesh,
        in_specs=placed,
        out_specs=(P("gx", "gy", None, None, None), P("gx", "gy", None)),
        check_vma=False,
    )
```

```python
import functools

import jax
import jax.numpy as jnp
from jax import lax
from jax.experimental import pallas as pl
from jax.experimental.pallas import tpu as pltpu
from jax.sharding import PartitionSpec as P

POWER_STEPS = 6
B = 128
SLOTS = 6
ORDER = SLOTS * B
MESH = pl.DeviceIdType.MESH
F32 = jnp.float32
BF16 = jnp.bfloat16

BELOW_X, ABOVE_X, BELOW_Y, ABOVE_Y = 1, 7, 3, 5
COPIES = 18 + 14 + 10

HIGH = 1
LOW = (0, 5, 4)


def split(value):
    high = value.astype(BF16)
    return high, (value - high.astype(F32)).astype(BF16)


class Exchange:
    def __init__(self, hood, sends, recvs, base, gx, gy, n_gx, n_gy, lows):
        odd = lax.rem(gx, 2)
        up_y = (gx, lax.rem(gy + 1, n_gy))
        down_y = (gx, lax.rem(gy + n_gy - 1, n_gy))
        step = 2 * odd - 1
        far = (lax.rem(gx + step + n_gx, n_gx), gy)
        near = (gx - step, gy)
        self.index = base

        def copy(source, target, rows, columns, device):
            index = self.index
            self.index += 1
            return pltpu.make_async_remote_copy(
                src_ref=hood.at[source, rows, columns],
                dst_ref=hood.at[target, rows, columns],
                send_sem=sends.at[index],
                recv_sem=recvs.at[index],
                device_id=device,
                device_id_type=MESH,
            )

        def planes(place, low):
            if not lows:
                return (1, 2) if place == BELOW_Y else (0, 1)
            if place == BELOW_Y:
                return (2, 3, 4) if low else (2, 3)
            return (1, 2, 0) if low else (1, 2)

        towards_far = pl.ds(2 * odd, 1)
        towards_near = pl.ds(2 - 2 * odd, 1)
        middle = pl.ds(1, 1)
        to_far, to_near = (far, -3 * step), (near, 3 * step)
        sides = ((BELOW_Y, up_y), (ABOVE_Y, down_y))
        self.steps = []

        def add(rows, targets, low, only_low=False):
            for which in range(3 if lows else 2):
                is_low = which == 2
                if is_low and not low or only_low and not is_low:
                    continue
                for place, device in sides:
                    plane = planes(place, True)[which]
                    columns = slice(plane, plane + 1)
                    arriving = copy(4, place, rows, columns, device)
                    going = [copy(place, place + shift, rows, columns, peer) for peer, shift in targets]
                    self.steps.append((arriving, going))

        add(middle, (to_far, to_near), False)
        add(towards_far, (to_far,), lows)
        add(towards_near, (to_near,), lows)
        if lows:
            add(middle, (), True, True)
        across = slice(1, 4) if lows else slice(0, 3)
        self.along_x = [
            copy(4, 4 - 3 * step, pl.ds(odd, 2), across, far),
            copy(4, 4 + 3 * step, pl.ds(1 - odd, 2), across, near),
        ]
        if lows:
            single = slice(LOW[1], LOW[1] + 1)
            self.along_x += [
                copy(4, 4 - 3 * step, towards_far, single, far),
                copy(4, 4 + 3 * step, towards_near, single, near),
            ]
        self.to_far = [c for n, (_, copies) in enumerate(self.steps) for c in copies[:1] if n < (10 if lows else 8)]
        self.to_near = [c for n, (_, copies) in enumerate(self.steps) for c in copies[-1:] if n < 4 or n >= (10 if lows else 8)]

    def begin(self, first, last):
        for arriving, _ in self.steps[first:last]:
            arriving.start()

    def begin_x(self):
        for copy in self.along_x:
            copy.start()

    def forward(self, first, last):
        for arriving, going in self.steps[first:last]:
            arriving.wait_recv()
            for copy in going:
                copy.start()

    def wait(self, copies):
        for copy in copies:
            copy.wait_recv()

    def wait_sent(self):
        for arriving, going in self.steps:
            arriving.wait_send()
            for copy in going:
                copy.wait_send()
        for copy in self.along_x:
            copy.wait_send()


def three(left, right):
    lhs = jnp.concatenate([left[0], left[0], left[1]], axis=1)
    rhs = jnp.concatenate([right[0], right[1], right[0]], axis=0)
    return jnp.dot(lhs, rhs, preferred_element_type=F32)


def thin(matrix, high, low):
    rhs = jnp.concatenate([high, low], axis=1)
    both = jnp.dot(matrix[0][...], rhs, preferred_element_type=F32)
    rest = jnp.dot(matrix[1][...], high, preferred_element_type=F32)
    return both[:, :B] + (both[:, B:] + rest)


def kernel(
    n_gx, n_gy,
    h_any, onsite_any, pattern_any, code_any, basis_any,
    density_ref, grid_ref,
    h_buf, onsite_ref, pattern_ref, code_ref, basis, hood, m_f, m_hi, m_lo, q_hi, q_lo, n_f, x_hi, x_lo,
    halves, dhood, grid_acc, best, best_x, best_y,
    in_sem, sends, recvs, sends_x, recvs_x, sends_y, recvs_y,
):
    gx, gy = lax.axis_index("gx"), lax.axis_index("gy")

    small = [
        pltpu.make_async_copy(source, target, in_sem.at[4 + n])
        for n, (source, target) in enumerate((
            (pattern_any, pattern_ref), (onsite_any, onsite_ref), (code_any, code_ref),
        ))
    ]
    loads = []
    for order, row in enumerate((1, 0, 2)):
        rows = pl.ds(3 * row, 3)
        loads.append(pltpu.make_async_copy(h_any.at[0, 0, rows], h_buf.at[rows], in_sem.at[order]))
    for copy in [loads[0]] + small:
        copy.start()
    barrier = pltpu.get_barrier_semaphore()
    for step in range(1, n_gx):
        pl.semaphore_signal(barrier, inc=1, device_id=(lax.rem(gx + step, n_gx), gy), device_id_type=MESH)
    for step in range(1, n_gy):
        pl.semaphore_signal(barrier, inc=1, device_id=(gx, lax.rem(gy + step, n_gy)), device_id_type=MESH)
    loads[1].start()
    loads[2].start()
    load_basis = pltpu.make_async_copy(basis_any.at[0, 0], basis, in_sem.at[3])
    load_basis.start()

    rows_of = lax.broadcasted_iota(jnp.int32, (B, B), 0)
    columns_of = lax.broadcasted_iota(jnp.int32, (B, B), 1)
    eye = rows_of == columns_of

    def prepare(row):
        for col in range(3):
            code = 3 * row + col
            block = h_buf[code]
            if code == 4:
                block = block + jnp.where(eye, onsite_ref[0], 0.0)
            else:
                block = block * pattern_ref[0, 0, code].astype(F32)
            high, low = split(block)
            hood[4, row, HIGH + col] = high
            hood[4, row, LOW[col]] = low

    swap = Exchange(hood, sends, recvs, 0, gx, gy, n_gx, n_gy, True)
    for copy in small + [loads[0]]:
        copy.wait()
    prepare(1)
    pl.semaphore_wait(barrier, n_gx + n_gy - 2)
    swap.begin(0, 4)
    loads[1].wait()
    prepare(0)
    loads[2].wait()
    prepare(2)
    swap.begin(4, 18)
    swap.begin_x()
    swap.forward(0, 18)
    swap.wait(swap.along_x + swap.to_near + swap.to_far)

    codes = [code_ref[0, 0, a] for a in range(SLOTS)]
    used = [code < 9 for code in codes]
    safe = [jnp.where(u, code, 4) for u, code in zip(used, codes)]
    off_x = [lax.div(s, 3) - 1 for s in safe]
    off_y = [lax.rem(s, 3) - 1 for s in safe]

    def stored(a, b):
        dx, dy = off_x[a] - off_x[b], off_y[a] - off_y[b]
        valid = (jnp.abs(dx) <= 1) & (jnp.abs(dy) <= 1) & used[a] & used[b]
        source = jnp.where(valid, safe[b], 4)
        row = jnp.where(valid, dx + 1, 1)
        col = jnp.where(valid, dy + 1, 1)
        block = hood[source, row, col + HIGH].astype(F32)
        if a == 0 or b == 0:
            plane = jnp.where(col == 1, LOW[1], jnp.where(col == 0, LOW[0], LOW[2]))
            block = block + hood[source, row, plane].astype(F32)
        return jnp.where(valid, block, 0.0)

    def put(a, b, block):
        place = (slice(a * B, a * B + B), slice(b * B, b * B + B))
        m_f[place] = block
        high, low = split(block)
        m_hi[place] = high
        m_lo[place] = low

    for a in range(SLOTS):
        block = stored(a, a)
        put(a, a, 0.5 * (block + block.T))
        for b in range(a + 1, SLOTS):
            upper = 0.5 * (stored(a, b) + stored(b, a).T)
            put(a, b, upper)
            put(b, a, upper.T)

    def from_rows(vector):
        out = []
        for b in range(SLOTS):
            total = jnp.zeros((8, B), F32)
            for a in range(SLOTS):
                part = m_f[a * B:a * B + B, b * B:b * B + B] * vector[a]
                total = total + jnp.sum(part.reshape(B // 8, 8, B), axis=0)
            out.append(jnp.sum(total, axis=0, keepdims=True))
        return out

    def from_lanes(vector):
        out = []
        for a in range(SLOTS):
            total = jnp.zeros((B, B), F32)
            for b in range(SLOTS):
                total = total + m_f[a * B:a * B + B, b * B:b * B + B] * vector[b]
            out.append(jnp.sum(total, axis=1, keepdims=True))
        return out

    def norm2(vector):
        total = sum(part * part for part in vector)
        return jnp.sum(total, keepdims=True)

    vector = [jnp.full((B, 1), 1.0, F32) * u.astype(F32) for u in used]
    length = jnp.ones((1, 1), F32)
    for step in range(POWER_STEPS + 1):
        image = from_rows(vector) if step % 2 == 0 else from_lanes(vector)
        total = norm2(image)
        factor = 1.0 / length
        if step < POWER_STEPS:
            vector = [part * factor for part in image]
            length = factor * jnp.sqrt(total + 1e-6 * (length * length))
    estimate = jnp.sqrt(total * (factor * factor) + 1e-6)
    best[0] = jnp.broadcast_to(estimate, (8, B))

    def share(source, target, sends_to, recvs_to, count, axis):
        out = []
        for step in range(1, count):
            peer = (lax.rem(gx + step, n_gx), gy) if axis == 0 else (gx, lax.rem(gy + step, n_gy))
            out.append(pltpu.make_async_remote_copy(
                src_ref=best.at[source],
                dst_ref=target.at[step - 1],
                send_sem=sends_to.at[step - 1],
                recv_sem=recvs_to.at[step - 1],
                device_id=peer,
                device_id_type=MESH,
            ))
        return out

    along_x = share(0, best_x, sends_x, recvs_x, n_gx, 0)
    along_y = share(1, best_y, sends_y, recvs_y, n_gy, 1)
    def apart(step, count, width):
        rows, row = divmod(step, width)
        lines = count // width
        return min(row, width - row) + min(rows, lines - rows)

    def start_all(group, count, width):
        for step in sorted(range(1, count), key=lambda n: -apart(n, count, width)):
            group[step - 1].start()

    start_all(along_x, n_gx, 2)

    for r in range(0, ORDER, 256):
        for c in range(r, ORDER, 256):
            rows, cols = slice(r, r + 256), slice(c, c + 256)
            block = three((m_hi[rows, :], m_lo[rows, :]), (m_hi[:, cols], m_lo[:, cols]))
            high, low = split(block)
            q_hi[rows, cols] = high
            q_lo[rows, cols] = low
            if r != c:
                high, low = split(block.T)
                q_hi[cols, rows] = high
                q_lo[cols, rows] = low

    top = best[0]
    for step, copy in enumerate(along_x):
        copy.wait_recv()
        top = jnp.maximum(top, best_x[step])
    best[1] = top
    start_all(along_y, n_gy, 4)

    for r in range(0, ORDER, 256):
        for c in range(r, ORDER, 256):
            rows, cols = slice(r, r + 256), slice(c, c + 256)
            block = three((m_hi[rows, :], m_lo[rows, :]), (q_hi[:, cols], q_lo[:, cols]))
            n_f[rows, cols] = block
            if r != c:
                n_f[cols, rows] = block.T

    powers = [m_f[:, :B], n_f[:, :B]]
    for _ in range(3):
        powers.append(thin((q_hi, q_lo), *split(powers[-1])))

    top = best[1]
    for step, copy in enumerate(along_y):
        copy.wait_recv()
        top = jnp.maximum(top, best_y[step])
    inverse = 1.0 / (1.25 * top[:1, :1])
    square = inverse * inverse

    alpha, beta = 1.5 * inverse, -0.5 * inverse * square
    for r in range(0, ORDER, B):
        rows = slice(r, r + B)
        high, low = split(alpha * m_f[rows, :] + beta * n_f[rows, :])
        x_hi[rows, :] = high
        x_lo[rows, :] = low
    weights = (
        2.25 * inverse,
        inverse * square * (-0.75 - 0.5 * 3.375),
        inverse * square * square * (0.5 * 3.375),
        inverse * square * square * square * (-0.5 * 1.125),
        inverse * square * square * square * square * (0.5 * 0.125),
    )
    second = sum(w * p for w, p in zip(weights, powers))

    def applied(value):
        once = thin((x_hi, x_lo), *split(value))
        twice = thin((x_hi, x_lo), *split(once))
        return 1.5 * once - 0.5 * thin((x_hi, x_lo), *split(twice))

    third = 1.5 * second - 0.5 * applied(applied(second))
    for a in range(SLOTS):
        block = -third[a * B:a * B + B]
        if a == 0:
            block = jnp.where(eye, 1.0, 0.0) + block
        halves[a] = 0.5 * block
    share_out = Exchange(dhood, sends, recvs, COPIES, gx, gy, n_gx, n_gy, False)
    for code in (3, 4, 5, 0, 1, 2, 6, 7, 8):
        slot = jnp.int32(0)
        held = codes[0] == code
        for a in range(1, SLOTS):
            slot = jnp.where(codes[a] == code, a, slot)
            held = held | (codes[a] == code)
        dhood[4, code // 3, code % 3] = jnp.where(held, halves[slot], 0.0).astype(BF16)
        if code == 5:
            share_out.begin(0, 4)
    share_out.begin(4, 12)
    share_out.begin_x()
    for code in range(9):
        density_ref[0, 0, code] = dhood[4, code // 3, code % 3]
    load_basis.wait()

    step = 2 * lax.rem(gx, 2) - 1

    def tile(near_x, near_y):
        fixed = isinstance(near_x, int)
        place = (near_x + 1) * 3 + near_y + 1
        if fixed:
            firsts = range(max(-near_x, 0), 3 - max(near_x, 0))
        else:
            start = lax.div(1 - near_x, 2)
            firsts = (start, start + 1)
        lefts, rights = [], []
        for row in firsts:
            for col in range(3):
                far_y = near_y + col - 1
                if abs(far_y) <= 1:
                    lefts.append((near_x + row) * 3 + far_y + 1)
                    rights.append(dhood[place, row, col])
        right = jnp.concatenate(rights, axis=0)

        def part(rows):
            left = jnp.concatenate([basis[e, rows, :] for e in lefts], axis=1)
            product = jnp.dot(left, right, preferred_element_type=F32)
            return product * basis[place, rows, :].astype(F32)

        return part

    points = grid_acc.shape[0]

    def add(near_x, near_y, first=False):
        part = tile(near_x, near_y)
        for start in range(0, points, 256):
            rows = slice(start, start + 256)
            grid_acc[rows, :] = part(rows) if first else grid_acc[rows, :] + part(rows)

    add(0, 0, True)
    share_out.forward(0, 4)
    share_out.wait(share_out.along_x)
    add(-1, 0)
    share_out.forward(4, 8)
    add(1, 0)
    share_out.forward(8, 12)
    add(0, -1)
    add(0, 1)
    share_out.wait(share_out.to_near)
    add(-step, -1)
    add(-step, 1)
    share_out.wait(share_out.to_far)
    parts = tile(step, -1), tile(step, 1)
    for start in range(0, points, 256):
        rows = slice(start, start + 256)
        block = grid_acc[rows, :] + (parts[0](rows) + parts[1](rows))
        for low in range(0, 256, B):
            grid_ref[0, :, pl.ds(start + low, B)] = jnp.sum(block[low:low + B].T, axis=0, keepdims=True)

    swap.wait_sent()
    share_out.wait_sent()
    for copy in along_x + along_y:
        copy.wait_send()


def write_out(density_in, grid_in, density_out, grid_out, sems):
    first = pltpu.make_async_copy(density_in, density_out, sems.at[0])
    second = pltpu.make_async_copy(grid_in, grid_out, sems.at[1])
    first.start()
    second.start()
    first.wait()
    second.wait()


def local(n_gx, n_gy, hblocks, onsite, pattern, slot_code, basis):
    points = basis.shape[3]
    total = COPIES
    hbm = pl.BlockSpec(memory_space=pltpu.HBM)
    vmem = pl.BlockSpec(memory_space=pltpu.VMEM)
    square = (ORDER, ORDER)
    hblocks, onsite, pattern, slot_code, basis = [
        pltpu.with_memory_space_constraint(x, pltpu.HBM)
        for x in (hblocks, onsite, pattern, slot_code, basis)
    ]
    density, grid = pl.pallas_call(
        functools.partial(kernel, n_gx, n_gy),
        out_shape=(
            jax.ShapeDtypeStruct((1, 1, 9, B, B), BF16),
            jax.ShapeDtypeStruct((1, 1, points), F32),
        ),
        in_specs=[hbm] * 5,
        out_specs=(vmem, vmem),
        scratch_shapes=[
            pltpu.VMEM((9, B, B), F32),
            pltpu.VMEM((1, 1, B), F32),
            pltpu.SMEM((1, 1, 9), jnp.int32),
            pltpu.SMEM((1, 1, SLOTS), jnp.int32),
            pltpu.VMEM((9, points, B), BF16),
            pltpu.VMEM((9, 3, 6, B, B), BF16),
            pltpu.VMEM(square, F32),
            pltpu.VMEM(square, BF16),
            pltpu.VMEM(square, BF16),
            pltpu.VMEM(square, BF16),
            pltpu.VMEM(square, BF16),
            pltpu.VMEM(square, F32),
            pltpu.VMEM(square, BF16),
            pltpu.VMEM(square, BF16),
            pltpu.VMEM((SLOTS, B, B), F32),
            pltpu.VMEM((9, 3, 3, B, B), BF16),
            pltpu.VMEM((points, B), F32),
            pltpu.VMEM((2, 8, B), F32),
            pltpu.VMEM((n_gx - 1, 8, B), F32),
            pltpu.VMEM((n_gy - 1, 8, B), F32),
            pltpu.SemaphoreType.DMA((7,)),
            pltpu.SemaphoreType.DMA((2 * total,)),
            pltpu.SemaphoreType.DMA((2 * total,)),
            pltpu.SemaphoreType.DMA((n_gx - 1,)),
            pltpu.SemaphoreType.DMA((n_gx - 1,)),
            pltpu.SemaphoreType.DMA((n_gy - 1,)),
            pltpu.SemaphoreType.DMA((n_gy - 1,)),
        ],
        compiler_params=pltpu.CompilerParams(
            collective_id=0, has_side_effects=True, vmem_limit_bytes=40 << 20
        ),
    )(hblocks, onsite, pattern, slot_code, basis)
    space = pl.BlockSpec(memory_space=pl.ANY)
    return pl.pallas_call(
        write_out,
        out_shape=(
            jax.ShapeDtypeStruct(density.shape, BF16),
            jax.ShapeDtypeStruct(grid.shape, F32),
        ),
        in_specs=[vmem, vmem],
        out_specs=(space, space),
        scratch_shapes=[pltpu.SemaphoreType.DMA((2,))],
    )(*[pltpu.with_memory_space_constraint(x, pltpu.VMEM) for x in (density, grid)])


def solution(mesh):
    placed = (
        P("gx", "gy", None, None, None),
        P("gx", "gy", None),
        P("gx", "gy", None),
        P("gx", "gy", None),
        P("gx", "gy", None, None, None),
    )
    return jax.shard_map(
        functools.partial(local, mesh.shape["gx"], mesh.shape["gy"]),
        mesh=mesh,
        in_specs=placed,
        out_specs=(P("gx", "gy", None, None, None), P("gx", "gy", None)),
        check_vma=False,
    )
```
